256 devices in a mesh: tm: 8 (over y, core), space: 32 (over x, z).
Axes of the slice: x: 4, y: 4, z: 8, core: 2. Of those that a mesh axis runs over, the one named last changes fastest.
Arguments:
- ensemble: bfloat16 [16, 64, 524288], P('tm', None, 'space'), may hold values from -6 to 6
- obs_owner: int32 [16, 4096, 1], P('tm', 'space'), may hold values from 0 to 31; in each aligned block of 128 rows (0 to 127, 128 to 255, ..., all dimensions but the last counted through in order) at most 8 rows name the same one
- obs_local: int32 [16, 4096], P('tm', 'space'), may hold values from 0 to 63
- obs_offset: int32 [16, 4096, 32], P('tm', 'space'), may hold values from 0 to 255
- obs_count: int32 [16, 4096], P('tm', 'space'), may hold values from 1 to 32
- obs_value: float32 [16, 4096, 32], P('tm', 'space'), may hold values from -12 to 12
- obs_var: float32 [16, 4096, 32], P('tm', 'space'), may hold values from 512 to 8192
- inflation: float32 [16], P('tm'), may hold values from 1.2 to 1.6
Outputs:
- smoothed: float32 [16, 64, 524288], P('tm', None, 'space')
The draws below stay inside these ranges and needn't reach their ends.
Inputs may be any that keep to these rules, and one draw needn't show every extreme that they name: `obs_owner`: in each window, the 128 observation blocks held by one index of space name any one owner at most 8 times, a bound that some block reaches.
All inputs are finite; a program needn't handle non-finite values.
Results may differ from the reference program's by a relative error of at most 0.0003.
Values may be sent and summed in bfloat16 or wider, within the bound.
No kernel may reach another device: no remote copies, remote signals or barrier semaphores. Data moves between devices by JAX's collectives and lax.ppermute only.
A program may use at most 64 MiB of HBM per device.

```python
import math
import jax
import jax.numpy as jnp
import numpy as np
from jax import lax

MEMB = 64
BLOCK = 256
SLOTS = 32
OBS_DEV = 128
NBLK_DEV = 64
CELLS = 524288
WINDOWS = 16
NOB = 4096
CAP = 8
N_SPACE = 32


def plant(entries, stream_key, low, largest):
    longest = entries.shape.index(max(entries.shape))
    spots = []
    for shift in (0, 1):
        where = [jax.random.randint(jax.random.fold_in(stream_key, axis), (), 0, length) for axis, length in enumerate(entries.shape)]
        where[longest] = (where[longest] + shift) % entries.shape[longest]
        spots.append(tuple(where))
    return entries.at[spots[0]].set(low).at[spots[1]].set(largest)


def level_of(key, dims, cuts, low, top_value):
    def one(position, blocks):
        heights = jax.random.uniform(jax.random.fold_in(jax.random.fold_in(key, 6), position), (blocks,), jnp.float32, low / len(cuts), top_value / len(cuts))
        return jnp.repeat(jnp.exp(heights), dims[position] // blocks).reshape((-1,) + (1,) * (len(dims) - position - 1))

    factor_of = one(*cuts[0])
    for cut in cuts[1:]:
        factor_of = factor_of * one(*cut)
    return factor_of


def deal_out(stream_key, own, number, rows, count, top, most, slope):
    ranking = jax.random.permutation(stream_key, count)
    heavy_load, usual = load_shares(count, rows * top, most, slope, True), load_shares(count, rows * top, most, slope, False)
    places = jnp.arange(count)

    def named(sizes, rotation):
        used = int((sizes > 0).sum())
        fixed = max(1, used // 4)
        passed = fixed + (places - fixed + rotation * (used - fixed)) % max(1, count - fixed)
        return jnp.zeros((count,), jnp.int32).at[ranking[jnp.where(places < fixed, places, passed)]].set(jnp.asarray(sizes, jnp.int32))

    sizes = jnp.where(number % 4 == 0, named(heavy_load, number // 4), named(usual, number - number // 4 - 1))
    mixed = jax.random.permutation(jax.random.fold_in(own, 3), count)
    source_of, sink = mixed[0:count // 2 * 2:2], mixed[1:count // 2 * 2:2]
    margin = jnp.minimum(sizes[source_of] - 1, most - sizes[sink]) // 2
    margin = jnp.where((source_of == ranking[0]) | (sink == ranking[0]) | (sizes[sink] == 0), 0, jnp.maximum(margin, 0))
    passed = jax.random.randint(jax.random.fold_in(own, 4), (count // 2,), 0, 1 << 20) % (margin + 1)
    sizes = sizes.at[source_of].add(-passed).at[sink].add(passed)
    labels = jnp.searchsorted(jnp.cumsum(sizes), jnp.arange(rows * top), side="right").astype(jnp.int32)
    table = labels.reshape(top, rows).T
    table = table[jax.random.permutation(jax.random.fold_in(own, 1), rows)]
    rotation = jax.random.randint(jax.random.fold_in(own, 2), (rows, 1), 0, top)
    return jnp.take_along_axis(table, (jnp.arange(top)[None, :] + rotation) % top, axis=1)


def load_shares(number_of, total, bound, skew, full):
    portions = [(1 << 20) // math.isqrt(grade ** skew) + 1 for grade in range(1, number_of + 1)]
    largest = bound if full else min(bound, max(-(-total // number_of), total * portions[0] // sum(portions)))
    least = 1 if total - largest >= number_of - 1 else 0
    counts, rest = [largest] + [least] * (number_of - 1), total - largest - least * (number_of - 1)
    while rest > 0:
        movable = [i for i in range(1, number_of) if counts[i] < largest] or [i for i in range(1, number_of) if counts[i] < bound]
        pool, remaining = sum([portions[i] for i in movable]), rest
        for i in movable:
            addition = min(bound - counts[i], max(1, remaining * portions[i] // pool), rest)
            counts[i] = counts[i] + addition
            rest = rest - addition
    return np.array(counts)


def scatter_about(stream_key, extent, spread, bound, shards=(), kind=jnp.bfloat16):
    drawn = jax.random.normal(stream_key, extent, jnp.float32) * spread
    if len(shards) > 0:
        drawn = level_of(stream_key, extent, shards, -0.22, 0.18) * drawn
    return jnp.clip(drawn, min=-bound, max=bound).astype(kind)


def setup_inputs(seed: int = 0) -> dict:
    keys = jax.random.split(jax.random.key(seed), 9)
    ensemble = scatter_about(keys[0], (WINDOWS, MEMB, CELLS), 1.0, 6.0, ((0, 8), (2, 32)))
    obs_owner_keys = jax.random.split(jax.random.fold_in(keys[1], 1), WINDOWS * NOB // OBS_DEV)
    obs_owner_turns = jax.random.permutation(jax.random.fold_in(keys[1], 3), WINDOWS * NOB // OBS_DEV)
    obs_owner = jax.vmap(lambda own, number: deal_out(jax.random.fold_in(keys[1], 2), own, number, OBS_DEV, N_SPACE, 1, CAP, 1))(obs_owner_keys, obs_owner_turns).reshape((WINDOWS, NOB, 1))
    obs_local = plant(jax.random.randint(keys[2], (WINDOWS, NOB), 0, NBLK_DEV), jax.random.fold_in(keys[2], 1), 0, NBLK_DEV - 1).astype(jnp.int32)
    obs_offset = plant(jax.random.randint(keys[3], (WINDOWS, NOB, SLOTS), 0, BLOCK), jax.random.fold_in(keys[3], 1), 0, BLOCK - 1).astype(jnp.int32)
    obs_count = plant(jax.random.randint(keys[4], (WINDOWS, NOB), 1, SLOTS + 1), jax.random.fold_in(keys[4], 1), 1, SLOTS).astype(jnp.int32)
    obs_value = scatter_about(keys[5], (WINDOWS, NOB, SLOTS), 3.0, 12.0, ((0, 8), (1, 32)), jnp.float32)
    obs_var = jnp.clip(jnp.exp(math.log(8192.0) - 2.7725887 * jax.random.uniform(keys[6], (WINDOWS, NOB, SLOTS), jnp.float32) ** level_of(keys[6], (WINDOWS, NOB, SLOTS), ((0, 8), (1, 32)), -0.2, 0.2)), 512.0, 8192.0)
    inflation = jnp.clip(jnp.exp(math.log(1.6) - 0.28768205 * jax.random.uniform(keys[7], (WINDOWS,), jnp.float32) ** level_of(keys[7], (WINDOWS,), ((0, 8),), -0.2, 0.2)), 1.2, 1.6)
    return {"ensemble": ensemble, "obs_owner": obs_owner, "obs_local": obs_local, "obs_offset": obs_offset, "obs_count": obs_count, "obs_value": obs_value, "obs_var": obs_var, "inflation": inflation}


def build_transform(gram_sum, projection, inflation):
    members = gram_sum.shape[-1]
    identity = jnp.eye(members, dtype=jnp.float32)
    system = (members - 1.0) * identity + gram_sum
    factor = jnp.linalg.cholesky(system)
    mean_weight = jax.scipy.linalg.cho_solve((factor, True), projection[..., None])
    inverse = jax.scipy.linalg.solve_triangular(factor, jnp.broadcast_to(identity, system.shape), lower=True)
    root_part = math.sqrt(members - 1.0) * jnp.swapaxes(inverse, -1, -2)
    center = identity - 1.0 / members
    inner = mean_weight + inflation[:, None, None] * root_part
    return 1.0 / members + jnp.matmul(center, inner, precision=lax.Precision.HIGHEST)

def window_stats(packed):
    members, owner_id, local_id, offset, slot_count, observed, error_var = packed
    blocks = owner_id[:, 0] * NBLK_DEV + local_id
    cell_index = (blocks[:, None] * BLOCK + offset).reshape(-1).astype(jnp.int32)
    picked = jnp.take(members, cell_index, axis=1).astype(jnp.float32)
    live_slot = jnp.arange(SLOTS, dtype=jnp.int32)[None, :] < slot_count[:, None]
    weight = jnp.where(live_slot, 1.0 / jnp.sqrt(error_var), jnp.float32(0.0)).reshape(-1)
    average = lax.optimization_barrier(jnp.mean(picked, axis=0))
    scaled = weight[None, :] * (picked - average[None, :])
    innovation = weight * (observed.reshape(-1) - average)
    gram_part = jnp.dot(scaled, scaled.T, precision=lax.Precision.HIGHEST)
    projection = jnp.dot(scaled, innovation, precision=lax.Precision.HIGHEST)
    return (gram_part, projection)

def apply_product(packed):
    members, product = packed
    return jnp.dot(product.T, members.astype(jnp.float32), precision=lax.Precision.HIGHEST)

def reference(ensemble, obs_owner, obs_local, obs_offset, obs_count, obs_value, obs_var, inflation):
    gram_sum, projection = lax.map(window_stats, (ensemble, obs_owner, obs_local, obs_offset, obs_count, obs_value, obs_var))
    transform = build_transform(gram_sum, projection, inflation)
    product = jnp.eye(MEMB, dtype=jnp.float32)
    suffixes = []
    for turn in range(WINDOWS - 1, -1, -1):
        product = jnp.matmul(transform[turn], product, precision=lax.Precision.HIGHEST)
        suffixes.insert(0, product)
    totals = jnp.stack(suffixes)
    return lax.map(apply_product, (ensemble, totals))
```

```python
import math

import jax
import jax.numpy as jnp
from jax import lax
from jax.experimental import pallas as pl
from jax.experimental.pallas import tpu as pltpu
from jax.sharding import PartitionSpec as P

MEMB = 64
BLOCK = 256
SLOTS = 32
CAP = 8
SHARDS = 32
NBLK = 64
CELLS = NBLK * BLOCK
ROWS = 40
STEP = 8
DEPTH = 4096
WIDTH = 4096

f32 = jnp.float32
bf16 = jnp.bfloat16
exact_mode = lax.Precision.HIGHEST
NT = (((1,), (1,)), ((), ()))


def iota(shape, dim):
    return lax.broadcasted_iota(jnp.int32, shape, dim)


def split(x):
    hi = x.astype(bf16)
    return hi, (x - hi.astype(f32)).astype(bf16)


def route_kernel(owner_ref, local_ref, offset_ref, count_ref, value_ref, var_ref, out_ref):
    for w in range(2):
        owner = owner_ref[w : w + 1, :]
        across = jnp.broadcast_to(owner, (128, 128))
        same = jnp.where((across == across.T) & (iota((128, 128), 0) < iota((128, 128), 1)), 1.0, 0.0)
        rank = jnp.sum(same, axis=0, keepdims=True).astype(jnp.int32)
        target = owner * CAP + rank
        placer = jnp.where(iota((SHARDS * CAP, 128), 0) == target, 1.0, 0.0).astype(bf16)
        live = iota((SLOTS, 128), 0) < count_ref[w : w + 1, :]
        precision = jnp.where(live, 1.0 / var_ref[w], 0.0)
        rows = jnp.concatenate(
            [
                precision,
                precision * value_ref[w],
                offset_ref[w].astype(f32),
                jnp.broadcast_to(local_ref[w : w + 1, :], (SLOTS, 128)).astype(f32),
            ],
            axis=0,
        )
        high = rows.astype(bf16)
        rest = rows - high.astype(f32)
        middle = rest.astype(bf16)
        low = (rest - middle.astype(f32)).astype(bf16)
        placed = sum(
            lax.dot_general(placer, part, NT, preferred_element_type=f32) for part in (low, middle, high)
        )
        out_ref[:, w * CAP : (w + 1) * CAP, :] = placed.reshape(SHARDS, CAP, 128)


def center_kernel(ens_hbm, mean_ref, ens, sems):
    copies = [
        pltpu.make_async_copy(
            ens_hbm.at[i // 4, :, pl.ds(i % 4 * 4096, 4096)], ens.at[i // 4, :, pl.ds(i % 4 * 4096, 4096)], sems.at[i]
        )
        for i in range(8)
    ]
    for copy in copies:
        copy.start()
    for i in range(8):
        copies[i].wait()

        def some(step, carry):
            block = i % 4 * 16 + step * 8
            for k in range(8):
                where = pl.ds(pl.multiple_of((block + k) * BLOCK, BLOCK), BLOCK)
                members = ens[i // 4, :, where].astype(f32)
                mean_ref[i // 4, pl.ds(block + k, 1), :] = jnp.sum(members, axis=0, keepdims=True) * (1.0 / MEMB)
            return carry

        lax.fori_loop(0, 2, some, 0)


def gram_kernel(recv_ref, mean_ref, ens_hbm, out_ref, ens, sems, table, dense, scale, ratio, scaled):
    copies = [pltpu.make_async_copy(ens_hbm.at[w], ens.at[w], sems.at[w]) for w in range(2)]
    for copy in copies:
        copy.start()
    for w in range(2):
        table[w] = recv_ref[:, w * CAP : (w + 1) * CAP, :].reshape(SHARDS * CAP, 128).T
    for w in range(2):

        def scatter(tile, carry):
            base = pl.multiple_of(tile * 32, 32)
            cells = (iota((32, 256), 0) + base).astype(f32)
            acc_u = jnp.zeros((32, 256), f32)
            acc_t = jnp.zeros((32, 256), f32)
            for s in range(SLOTS):
                hit = table[w, 64 + s : 65 + s, :] == cells
                acc_u += jnp.where(hit, table[w, s : s + 1, :], 0.0)
                acc_t += jnp.where(hit, table[w, 32 + s : 33 + s, :], 0.0)
            dense[w, pl.ds(base, 32), :] = acc_u
            dense[w, pl.ds(base + 256, 32), :] = acc_t
            return carry

        lax.fori_loop(0, 8, scatter, 0)
    for w in range(2):
        held = jnp.where(iota((NBLK, 256), 0).astype(f32) == table[w, 96:97, :], 1.0, 0.0).astype(bf16)
        placed = sum(lax.dot_general(held, part, NT, preferred_element_type=f32) for part in split(dense[w])[::-1])
        total = placed[:, :256]
        root = jnp.sqrt(total)
        scale[w] = root
        ratio[w] = jnp.where(total > 0.0, (placed[:, 256:] - total * mean_ref[w]) / root, 0.0)
    row16 = iota((16, BLOCK), 0)
    fulls = []
    for w in range(2):
        copies[w].wait()

        def fill(step, carry):
            for k in range(8):
                b = step * 8 + k
                where = pl.ds(pl.multiple_of(b * BLOCK, BLOCK), BLOCK)
                deviations = ens[w, :, where].astype(f32) - mean_ref[w, pl.ds(b, 1), :]
                high, low = split(deviations * scale[w, pl.ds(b, 1), :])
                scaled[w, 16 : 16 + MEMB, where] = high
                scaled[w, 16 + MEMB :, where] = low
                extra = ratio[w, pl.ds(b, 1), :]
                top = extra.astype(bf16).astype(f32)
                scaled[w, 0:16, where] = jnp.where(
                    row16 == 0, top, jnp.where(row16 == 1, extra - top, 0.0)
                ).astype(bf16)
            return carry

        lax.fori_loop(0, NBLK // 8, fill, 0)

        def product(step, acc):
            where = pl.ds(pl.multiple_of(step * DEPTH, DEPTH), DEPTH)
            return acc + lax.dot_general(
                scaled[w, 16:, where], scaled[w, : MEMB + 16, where], NT, preferred_element_type=f32
            )

        fulls.append(lax.fori_loop(0, CELLS // DEPTH, product, jnp.zeros((2 * MEMB, MEMB + 16), f32)))
    packs = []
    for full in fulls:
        cross = full[MEMB:, 16:]
        gram = full[:MEMB, 16:] + (cross + cross.T)
        both = full[:MEMB] + full[MEMB:]
        packs.append((gram, both[:, :1] + both[:, 1:2]))
    row, col = iota((MEMB, MEMB), 0), iota((MEMB, MEMB), 1)

    def as_row(values):
        return jnp.sum(jnp.where(row == col, values, 0.0), axis=0, keepdims=True)

    mixed = jnp.where(row <= col, packs[0][0], packs[1][0])
    body = jnp.concatenate([mixed[:32], mixed[32:]], axis=1)
    first = jnp.concatenate([as_row(packs[1][0]), as_row(packs[0][1])], axis=1)
    second = jnp.concatenate([as_row(packs[1][1]), jnp.zeros((1, MEMB), f32)], axis=1)
    packed = jnp.concatenate([body, first, second, jnp.zeros((ROWS - 34, 128), f32)], axis=0)
    out_ref[...] = jnp.broadcast_to(packed[None], (SHARDS, ROWS, 128))


def eliminate(systems):
    row, lane = iota((MEMB, 2 * MEMB), 0), iota((MEMB, 2 * MEMB), 1)
    eye = jnp.where(row + MEMB == lane, 1.0, 0.0)
    count = len(systems)
    tiles = []
    for system in systems:
        wide = jnp.concatenate([system, jnp.zeros((MEMB, MEMB), f32)], axis=1) + eye
        tiles.append([wide[8 * i : 8 * i + 8] for i in range(MEMB // 8)])
    found = [[] for _ in systems]
    full = (8, 2 * MEMB)
    for j in range(0, MEMB, STEP):
        t, s = divmod(j, 8)
        for w in range(count):
            rows = [jnp.broadcast_to(tiles[w][t][s + k : s + k + 1, :], full) for k in range(STEP)]
            block = [
                [jnp.broadcast_to(rows[k][:, j + l : j + l + 1], full) if l >= k else None for l in range(STEP)]
                for k in range(STEP)
            ]
            inverses, lower = [], [[None] * STEP for _ in range(STEP)]
            for k in range(STEP):
                inv = 1.0 / block[k][k]
                inverses.append(inv)
                for l in range(k + 1, STEP):
                    lower[l][k] = block[k][l] * inv
                for l in range(k + 1, STEP):
                    for m in range(l, STEP):
                        block[l][m] = block[l][m] - lower[l][k] * block[k][m]
                    rows[l] = rows[l] - lower[l][k] * rows[k]
            for k in range(STEP):
                found[w].append(rows[k][:1, :] * lax.rsqrt(block[k][k][:1, :]))
            first = t if s + STEP < 8 else t + 1
            if first == MEMB // 8:
                continue
            solved = [None] * STEP
            for k in reversed(range(STEP)):
                value = rows[k] * inverses[k]
                for l in range(k + 1, STEP):
                    value = value - lower[l][k] * solved[l]
                solved[k] = value
            for i in range(first, MEMB // 8):
                tile = tiles[w][i]
                change = None
                for k in range(STEP):
                    part = jnp.broadcast_to(tile[:, j + k : j + k + 1], full) * solved[k]
                    change = part if change is None else change + part
                tiles[w][i] = tile - change
    return [jnp.concatenate(rows, axis=0)[:, MEMB:] for rows in found]


def transform_kernel(infl_ref, parts_ref, out_ref, product_ref):
    total = jnp.sum(parts_ref[...], axis=0)
    mixed = jnp.concatenate([total[:32, :MEMB], total[:32, MEMB:]], axis=0)
    other = mixed.T
    row, col = iota((MEMB, MEMB), 0), iota((MEMB, MEMB), 1)
    diag = jnp.where(row == col, total[32:33, :MEMB], 0.0)
    grams = [jnp.where(row <= col, mixed, other), jnp.where(row > col, mixed, jnp.where(row < col, other, diag))]
    projs = [total[32:33, MEMB:], total[33:34, :MEMB]]
    ridge = jnp.where(row == col, MEMB - 1.0, 0.0)
    result = []
    for w, inverse in enumerate(eliminate([gram + ridge for gram in grams])):
        half = jnp.sum(inverse * projs[w], axis=1, keepdims=True)
        weight = jnp.sum(inverse * half, axis=0, keepdims=True)
        inner = weight + (infl_ref[w] * math.sqrt(MEMB - 1.0)) * inverse
        result.append(1.0 / MEMB + inner - jnp.sum(inner, axis=1, keepdims=True) * (1.0 / MEMB))
    out_ref[0] = result[0]
    out_ref[1] = result[1]
    product_ref[...] = exact(result[1], result[0])


def exact(a, b):
    return jnp.dot(a, b, precision=exact_mode, preferred_element_type=f32)


def apply_kernel(suffix_ref, made_ref, ens_hbm, out_hbm, ens, out, in_sems, out_sems):
    pieces = 16384 // WIDTH

    def part(i):
        return (i // pieces, slice(None), pl.ds(i % pieces * WIDTH, WIDTH))

    reads = [pltpu.make_async_copy(ens_hbm.at[part(i)], ens.at[i], in_sems.at[i]) for i in range(2 * pieces)]
    for copy in reads:
        copy.start()
    last = exact(suffix_ref[...], made_ref[1])
    totals = [exact(last, made_ref[0]), last]
    writes = []
    for i in range(2 * pieces):
        reads[i].wait()
        both = jnp.concatenate(split(totals[i // pieces]), axis=1)
        cells = ens[i]
        out[i] = jnp.dot(both, jnp.concatenate([cells, cells], axis=0), preferred_element_type=f32)
        writes.append(pltpu.make_async_copy(out.at[i], out_hbm.at[part(i)], out_sems.at[i]))
        writes[i].start()
    for copy in writes:
        copy.wait()


def times(a, b):
    return jnp.matmul(a, b, precision=exact_mode)


def body(ensemble, obs_owner, obs_local, obs_offset, obs_count, obs_value, obs_var, inflation):
    vmem = pl.BlockSpec(memory_space=pltpu.VMEM)
    turned = lambda a: jnp.swapaxes(a, 1, 2)
    routed = pl.pallas_call(
        route_kernel,
        out_shape=pltpu.VMEM((SHARDS, 2 * CAP, 128), f32),
        in_specs=[vmem] * 6,
        out_specs=vmem,
        name="route",
    )(obs_owner[:, :, 0], obs_local, turned(obs_offset), obs_count, turned(obs_value), turned(obs_var))
    recv = lax.all_to_all(routed, "space", split_axis=0, concat_axis=0, tiled=True)
    ensemble = pltpu.with_memory_space_constraint(ensemble, pltpu.HBM)
    means = pl.pallas_call(
        center_kernel,
        out_shape=pltpu.VMEM((2, NBLK, BLOCK), f32),
        in_specs=[pl.BlockSpec(memory_space=pl.ANY)],
        out_specs=vmem,
        scratch_shapes=[pltpu.VMEM((2, MEMB, CELLS), bf16), pltpu.SemaphoreType.DMA((8,))],
        compiler_params=pltpu.CompilerParams(vmem_limit_bytes=20 * 2**20),
        name="center",
    )(ensemble)
    partial = pl.pallas_call(
        gram_kernel,
        out_shape=pltpu.VMEM((SHARDS, ROWS, 128), f32),
        in_specs=[vmem, vmem, pl.BlockSpec(memory_space=pl.ANY)],
        out_specs=vmem,
        scratch_shapes=[
            pltpu.VMEM((2, MEMB, CELLS), bf16),
            pltpu.SemaphoreType.DMA((2,)),
            pltpu.VMEM((2, 128, 256), f32),
            pltpu.VMEM((2, 512, 256), f32),
            pltpu.VMEM((2, NBLK, BLOCK), f32),
            pltpu.VMEM((2, NBLK, BLOCK), f32),
            pltpu.VMEM((2, 2 * MEMB + 16, CELLS), bf16),
        ],
        compiler_params=pltpu.CompilerParams(vmem_limit_bytes=30 * 2**20),
        name="gram",
    )(recv, means, ensemble)
    parts = lax.all_to_all(partial, "space", split_axis=0, concat_axis=0, tiled=True)
    made, product = pl.pallas_call(
        transform_kernel,
        out_shape=(pltpu.VMEM((2, MEMB, MEMB), f32), pltpu.VMEM((MEMB, MEMB), f32)),
        in_specs=[pl.BlockSpec(memory_space=pltpu.SMEM), vmem],
        out_specs=(vmem, vmem),
        compiler_params=pltpu.CompilerParams(vmem_limit_bytes=20 * 2**20),
        name="transform",
    )(inflation, parts)
    place = lax.axis_index("tm")
    eye = jnp.eye(MEMB, dtype=f32)
    suffix = eye
    for bit in (1, 2, 4):
        other = lax.ppermute(product, "tm", [(i, i ^ bit) for i in range(8)])
        first = (place & bit) == 0
        ahead = jnp.where(first, other, eye)
        suffix = ahead if bit == 1 else times(ahead, suffix)
        if bit < 4:
            product = times(jnp.where(first, other, product), jnp.where(first, product, other))
    return pl.pallas_call(
        apply_kernel,
        out_shape=jax.ShapeDtypeStruct((2, MEMB, CELLS), f32),
        in_specs=[vmem, vmem, pl.BlockSpec(memory_space=pl.ANY)],
        out_specs=pl.BlockSpec(memory_space=pl.ANY),
        scratch_shapes=[
            pltpu.VMEM((2 * CELLS // WIDTH, MEMB, WIDTH), bf16),
            pltpu.VMEM((2 * CELLS // WIDTH, MEMB, WIDTH), f32),
            pltpu.SemaphoreType.DMA((2 * CELLS // WIDTH,)),
            pltpu.SemaphoreType.DMA((2 * CELLS // WIDTH,)),
        ],
        compiler_params=pltpu.CompilerParams(vmem_limit_bytes=30 * 2**20),
        name="apply",
    )(suffix, made, ensemble)


def solution(mesh):
    in_specs = (
        P("tm", None, "space"),
        P("tm", "space", None),
        P("tm", "space"),
        P("tm", "space", None),
        P("tm", "space"),
        P("tm", "space", None),
        P("tm", "space", None),
        P("tm"),
    )
    out_specs = P("tm", None, "space")
    return jax.shard_map(body, mesh=mesh, in_specs=in_specs, out_specs=out_specs, check_vma=False)
```

```python
import math

import jax
import jax.numpy as jnp
from jax import lax
from jax.experimental import pallas as pl
from jax.experimental.pallas import tpu as pltpu
from jax.sharding import PartitionSpec as P

MEMB = 64
BLOCK = 256
SLOTS = 32
SHARDS = 32
NBLK = 64
CELLS = NBLK * BLOCK
HALF = MEMB // 2
STEP = 8
WIDTH = 4096

f32 = jnp.float32
bf16 = jnp.bfloat16
exact_mode = lax.Precision.HIGHEST
NT = (((1,), (1,)), ((), ()))


def iota(shape, dim):
    return lax.broadcasted_iota(jnp.int32, shape, dim)


def split(x):
    hi = x.astype(bf16)
    return hi, (x - hi.astype(f32)).astype(bf16)


def route_kernel(owner_ref, local_ref, offset_ref, count_ref, value_ref, var_ref, out_ref):
    for w in range(2):
        owner = owner_ref[w : w + 1, :]
        across = jnp.broadcast_to(owner, (128, 128))
        same = jnp.where((across == across.T) & (iota((128, 128), 0) < iota((128, 128), 1)), 1.0, 0.0)
        rank = jnp.sum(same, axis=0, keepdims=True).astype(jnp.int32)
        target = owner * 2 + rank // 4
        placer = jnp.where(iota((2 * SHARDS, 128), 0) == target, 1.0, 0.0).astype(bf16)
        live = iota((SLOTS, 128), 0) < count_ref[w : w + 1, :]
        precision = jnp.where(live, 1.0 / var_ref[w], 0.0)
        rows = jnp.concatenate(
            [precision, precision * value_ref[w], (local_ref[w : w + 1, :] * BLOCK + offset_ref[w]).astype(f32)],
            axis=0,
        )
        wide = jnp.concatenate(
            [
                jnp.where(rank % 4 == c, rows[SLOTS * q : SLOTS * q + SLOTS], 0.0)
                for q in range(3)
                for c in range(4)
            ],
            axis=0,
        )
        high = wide.astype(bf16)
        rest = wide - high.astype(f32)
        middle = rest.astype(bf16)
        low = (rest - middle.astype(f32)).astype(bf16)
        placed = sum(
            lax.dot_general(placer, part, NT, preferred_element_type=f32) for part in (low, middle, high)
        )
        for q in range(3):
            out_ref[:, q, 2 * w : 2 * w + 2, :] = placed[:, 128 * q : 128 * q + 128].reshape(SHARDS, 2, 128)


def center_kernel(ens_hbm, mean_ref, ens, sems):
    copies = [
        pltpu.make_async_copy(
            ens_hbm.at[i // 4, :, pl.ds(i % 4 * 4096, 4096)], ens.at[i // 4, :, pl.ds(i % 4 * 4096, 4096)], sems.at[i]
        )
        for i in range(8)
    ]
    for copy in copies:
        copy.start()
    for i in range(8):
        copies[i].wait()

        def some(step, carry):
            block = i % 4 * 16 + step * 8
            for k in range(8):
                where = pl.ds(pl.multiple_of((block + k) * BLOCK, BLOCK), BLOCK)
                members = ens[i // 4, :, where].astype(f32)
                mean_ref[i // 4, pl.ds(block + k, 1), :] = jnp.sum(members, axis=0, keepdims=True) * (1.0 / MEMB)
            return carry

        lax.fori_loop(0, 2, some, 0)


def gram_kernel(recv_ref, mean_ref, ens_hbm, out_ref, ens, sems, table, dense, scale, ratio, even, odd, sums):
    copies = [pltpu.make_async_copy(ens_hbm.at[w], ens.at[w], sems.at[w]) for w in range(2)]
    for copy in copies:
        copy.start()
    for q in range(3):
        table[q] = jnp.concatenate(
            [recv_ref[:, q, 2 * w : 2 * w + 2, :].reshape(2 * SHARDS, 128) for w in range(2)], axis=0
        ).T
    locals_ = []
    for c in range(4):
        held = jnp.floor(table[2, SLOTS * c : SLOTS * c + 1, :] * (1.0 / BLOCK))
        locals_.append(held)
        table[2, SLOTS * c : SLOTS * c + SLOTS, :] = table[2, SLOTS * c : SLOTS * c + SLOTS, :] - held * BLOCK

    def scatter(tile, carry):
        base = pl.multiple_of(tile * 32, 32)
        cells = (iota((32, 128), 0) + base).astype(f32)
        for c in range(4):
            acc_u = jnp.zeros((32, 128), f32)
            acc_t = jnp.zeros((32, 128), f32)
            for r in range(SLOTS * c, SLOTS * c + SLOTS):
                hit = table[2, r : r + 1, :] == cells
                acc_u += jnp.where(hit, table[0, r : r + 1, :], 0.0)
                acc_t += jnp.where(hit, table[1, r : r + 1, :], 0.0)
            dense[pl.ds(base, 32), 128 * c : 128 * c + 128] = acc_u
            dense[pl.ds(base + 256, 32), 128 * c : 128 * c + 128] = acc_t
        return carry

    lax.fori_loop(0, 8, scatter, 0)
    row, lane = iota((2 * NBLK, 128), 0), iota((2 * NBLK, 128), 1)
    ours = (row // NBLK) == (lane // NBLK)
    holder = jnp.concatenate(
        [jnp.where(ours & ((row % NBLK).astype(f32) == held), 1.0, 0.0) for held in locals_], axis=1
    ).astype(bf16)
    placed = sum(lax.dot_general(holder, part, NT, preferred_element_type=f32) for part in split(dense[...])[::-1])
    for w in range(2):
        total = placed[NBLK * w : NBLK * w + NBLK, :256]
        root = jnp.sqrt(total)
        scale[w] = root
        ratio[w] = jnp.where(
            total > 0.0, (placed[NBLK * w : NBLK * w + NBLK, 256:] - total * mean_ref[w]) / root, 0.0
        )
    row16 = iota((16, BLOCK), 0)

    def fill(ref, step):
        w = step // 8
        for k in range(8):
            b = step % 8 * 8 + k
            here = slice(BLOCK * k, BLOCK * k + BLOCK)
            cells = ens[w, :, pl.ds(pl.multiple_of(b * BLOCK, BLOCK), BLOCK)].astype(f32)
            high, low = split((cells - mean_ref[w, pl.ds(b, 1), :]) * scale[w, pl.ds(b, 1), :])
            ref[16 : 16 + MEMB, here] = high
            ref[16 + MEMB :, here] = low
            extra = ratio[w, pl.ds(b, 1), :]
            top = extra.astype(bf16).astype(f32)
            ref[0:16, here] = jnp.where(row16 == 0, top, jnp.where(row16 == 1, extra - top, 0.0)).astype(bf16)

    def product(ref, step):
        w = step // 8
        sums[w] = sums[w] + lax.dot_general(ref[16:, :], ref[: MEMB + 16, :], NT, preferred_element_type=f32)

    def steps(i, carry):
        product(even, 2 * i)
        fill(odd, 2 * i + 1)
        product(odd, 2 * i + 1)
        fill(even, jnp.minimum(2 * i + 2, 15))
        return carry

    sums[...] = jnp.zeros((2, 2 * MEMB, MEMB + 16), f32)
    for copy in copies:
        copy.wait()
    fill(even, 0)
    lax.fori_loop(0, 8, steps, 0)
    row, col = iota((MEMB, MEMB), 0), iota((MEMB, MEMB), 1)
    lines = []
    for w in range(2):
        full = sums[w]
        cross = full[MEMB:, 16:]
        gram = full[:MEMB, 16:] + (cross + cross.T)
        both = full[:MEMB] + full[MEMB:]
        proj = jnp.sum(jnp.where(row == col, both[:, :1] + both[:, 1:2], 0.0), axis=0, keepdims=True)
        diag = jnp.sum(jnp.where(row == col, gram, 0.0), axis=0, keepdims=True)
        mixed = jnp.where(row[:HALF, :HALF] <= col[:HALF, :HALF], gram[:HALF, :HALF], gram[HALF:, HALF:])
        halves = jnp.concatenate([mixed, gram[:HALF, HALF:]], axis=1)
        body = jnp.concatenate([halves[:16], halves[16:]], axis=1)
        last = jnp.concatenate([proj, diag], axis=1)
        lines.append(jnp.concatenate([body[r : r + 1] for r in range(16)] + [last], axis=1))
    for d in range(SHARDS):
        out_ref[d] = lines[d % 2]


def eliminate(systems):
    row, lane = iota((MEMB, 2 * MEMB), 0), iota((MEMB, 2 * MEMB), 1)
    eye = jnp.where(row + MEMB == lane, 1.0, 0.0)
    count = len(systems)
    tiles = []
    for system in systems:
        wide = jnp.concatenate([system, jnp.zeros((MEMB, MEMB), f32)], axis=1) + eye
        tiles.append([wide[8 * i : 8 * i + 8] for i in range(MEMB // 8)])
    found = [[] for _ in systems]
    full = (8, 2 * MEMB)
    for j in range(0, MEMB, STEP):
        t, s = divmod(j, 8)
        for w in range(count):
            rows = [jnp.broadcast_to(tiles[w][t][s + k : s + k + 1, :], full) for k in range(STEP)]
            block = [
                [jnp.broadcast_to(rows[k][:, j + l : j + l + 1], full) if l >= k else None for l in range(STEP)]
                for k in range(STEP)
            ]
            inverses, lower = [], [[None] * STEP for _ in range(STEP)]
            for k in range(STEP):
                inv = 1.0 / block[k][k]
                inverses.append(inv)
                for l in range(k + 1, STEP):
                    lower[l][k] = block[k][l] * inv
                for l in range(k + 1, STEP):
                    for m in range(l, STEP):
                        block[l][m] = block[l][m] - lower[l][k] * block[k][m]
                    rows[l] = rows[l] - lower[l][k] * rows[k]
            for k in range(STEP):
                found[w].append(rows[k][:1, :] * lax.rsqrt(block[k][k][:1, :]))
            first = t if s + STEP < 8 else t + 1
            if first == MEMB // 8:
                continue
            solved = [None] * STEP
            for k in reversed(range(STEP)):
                value = rows[k] * inverses[k]
                for l in range(k + 1, STEP):
                    value = value - lower[l][k] * solved[l]
                solved[k] = value
            for i in range(first, MEMB // 8):
                tile = tiles[w][i]
                change = None
                for k in range(STEP):
                    part = jnp.broadcast_to(tile[:, j + k : j + k + 1], full) * solved[k]
                    change = part if change is None else change + part
                tiles[w][i] = tile - change
    return [jnp.concatenate(rows, axis=0)[:, MEMB:] for rows in found]


def transform_kernel(infl_ref, parts_ref, out_ref):
    total = jnp.sum(parts_ref[...], axis=0)
    body = jnp.concatenate([total[:, 128 * r : 128 * r + 128] for r in range(16)], axis=0)
    proj = total[:, 2048 : 2048 + MEMB]
    halves = jnp.concatenate([body[:, :MEMB], body[:, MEMB:]], axis=0)
    mixed, corner = halves[:, :HALF], halves[:, HALF:]
    other = mixed.T
    row, col = iota((HALF, HALF), 0), iota((HALF, HALF), 1)
    diag = jnp.where(row == col, total[:, 2048 + MEMB + HALF : 2048 + 2 * MEMB], 0.0)
    upper = jnp.where(row <= col, mixed, other)
    under = jnp.where(row > col, mixed, jnp.where(row < col, other, diag))
    gram = jnp.concatenate(
        [jnp.concatenate([upper, corner], axis=1), jnp.concatenate([corner.T, under], axis=1)], axis=0
    )
    ridge = jnp.where(iota((MEMB, MEMB), 0) == iota((MEMB, MEMB), 1), MEMB - 1.0, 0.0)
    inverse = eliminate([gram + ridge])[0]
    half = jnp.sum(inverse * proj, axis=1, keepdims=True)
    weight = jnp.sum(inverse * half, axis=0, keepdims=True)
    inner = weight + (infl_ref[0] * math.sqrt(MEMB - 1.0)) * inverse
    out_ref[...] = 1.0 / MEMB + inner - jnp.sum(inner, axis=1, keepdims=True) * (1.0 / MEMB)


def exact(a, b):
    return jnp.dot(a, b, precision=exact_mode, preferred_element_type=f32)


def apply_kernel(suffix_ref, first_ref, second_ref, ens_hbm, out_hbm, ens, out, in_sems, out_sems):
    pieces = 16384 // WIDTH

    def part(i):
        return (i // pieces, slice(None), pl.ds(i % pieces * WIDTH, WIDTH))

    reads = [pltpu.make_async_copy(ens_hbm.at[part(i)], ens.at[i], in_sems.at[i]) for i in range(2 * pieces)]
    for copy in reads:
        copy.start()
    last = exact(suffix_ref[...], second_ref[...])
    totals = [exact(last, first_ref[...]), last]
    writes = []
    for i in range(2 * pieces):
        reads[i].wait()
        both = jnp.concatenate(split(totals[i // pieces]), axis=1)
        cells = ens[i]
        out[i] = jnp.dot(both, jnp.concatenate([cells, cells], axis=0), preferred_element_type=f32)
        writes.append(pltpu.make_async_copy(out.at[i], out_hbm.at[part(i)], out_sems.at[i]))
        writes[i].start()
    for copy in writes:
        copy.wait()


def times(a, b):
    return jnp.matmul(a, b, precision=exact_mode)


def body(ensemble, obs_owner, obs_local, obs_offset, obs_count, obs_value, obs_var, inflation):
    vmem = pl.BlockSpec(memory_space=pltpu.VMEM)
    turned = lambda a: jnp.swapaxes(a, 1, 2)
    routed = pl.pallas_call(
        route_kernel,
        out_shape=pltpu.VMEM((SHARDS, 3, 4, 128), f32),
        in_specs=[vmem] * 6,
        out_specs=vmem,
        name="route",
    )(obs_owner[:, :, 0], obs_local, turned(obs_offset), obs_count, turned(obs_value), turned(obs_var))
    recv = lax.all_to_all(routed, "space", split_axis=0, concat_axis=0, tiled=True)
    ensemble = pltpu.with_memory_space_constraint(ensemble, pltpu.HBM)
    means = pl.pallas_call(
        center_kernel,
        out_shape=pltpu.VMEM((2, NBLK, BLOCK), f32),
        in_specs=[pl.BlockSpec(memory_space=pl.ANY)],
        out_specs=vmem,
        scratch_shapes=[pltpu.VMEM((2, MEMB, CELLS), bf16), pltpu.SemaphoreType.DMA((8,))],
        compiler_params=pltpu.CompilerParams(vmem_limit_bytes=20 * 2**20),
        name="center",
    )(ensemble)
    partial = pl.pallas_call(
        gram_kernel,
        out_shape=pltpu.VMEM((SHARDS, 1, 2176), f32),
        in_specs=[vmem, vmem, pl.BlockSpec(memory_space=pl.ANY)],
        out_specs=vmem,
        scratch_shapes=[
            pltpu.VMEM((2, MEMB, CELLS), bf16),
            pltpu.SemaphoreType.DMA((2,)),
            pltpu.VMEM((3, 128, 128), f32),
            pltpu.VMEM((512, 512), f32),
            pltpu.VMEM((2, NBLK, BLOCK), f32),
            pltpu.VMEM((2, NBLK, BLOCK), f32),
            pltpu.VMEM((2 * MEMB + 16, 8 * BLOCK), bf16),
            pltpu.VMEM((2 * MEMB + 16, 8 * BLOCK), bf16),
            pltpu.VMEM((2, 2 * MEMB, MEMB + 16), f32),
        ],
        compiler_params=pltpu.CompilerParams(vmem_limit_bytes=30 * 2**20),
        name="gram",
    )(recv, means, ensemble)
    parts = lax.all_to_all(partial, "space", split_axis=0, concat_axis=0, tiled=True)
    second = (lax.axis_index("space") & 1) == 1
    made = pl.pallas_call(
        transform_kernel,
        out_shape=pltpu.VMEM((MEMB, MEMB), f32),
        in_specs=[pl.BlockSpec(memory_space=pltpu.SMEM), vmem],
        out_specs=vmem,
        compiler_params=pltpu.CompilerParams(vmem_limit_bytes=20 * 2**20),
        name="transform",
    )(jnp.where(second, inflation[1:], inflation[:1]), parts)
    paired = lax.ppermute(made, "space", [(i, i ^ 1) for i in range(SHARDS)])
    early, late = jnp.where(second, paired, made), jnp.where(second, made, paired)
    product = times(late, early)
    place = lax.axis_index("tm")
    eye = jnp.eye(MEMB, dtype=f32)
    suffix = eye
    for bit in (1, 2, 4):
        other = lax.ppermute(product, "tm", [(i, i ^ bit) for i in range(8)])
        first = (place & bit) == 0
        ahead = jnp.where(first, other, eye)
        suffix = ahead if bit == 1 else times(ahead, suffix)
        if bit < 4:
            product = times(jnp.where(first, other, product), jnp.where(first, product, other))
    return pl.pallas_call(
        apply_kernel,
        out_shape=jax.ShapeDtypeStruct((2, MEMB, CELLS), f32),
        in_specs=[vmem, vmem, vmem, pl.BlockSpec(memory_space=pl.ANY)],
        out_specs=pl.BlockSpec(memory_space=pl.ANY),
        scratch_shapes=[
            pltpu.VMEM((2 * CELLS // WIDTH, MEMB, WIDTH), bf16),
            pltpu.VMEM((2 * CELLS // WIDTH, MEMB, WIDTH), f32),
            pltpu.SemaphoreType.DMA((2 * CELLS // WIDTH,)),
            pltpu.SemaphoreType.DMA((2 * CELLS // WIDTH,)),
        ],
        compiler_params=pltpu.CompilerParams(vmem_limit_bytes=30 * 2**20),
        name="apply",
    )(suffix, early, late, ensemble)


def solution(mesh):
    in_specs = (
        P("tm", None, "space"),
        P("tm", "space", None),
        P("tm", "space"),
        P("tm", "space", None),
        P("tm", "space"),
        P("tm", "space", None),
        P("tm", "space", None),
        P("tm"),
    )
    out_specs = P("tm", None, "space")
    return jax.shard_map(body, mesh=mesh, in_specs=in_specs, out_specs=out_specs, check_vma=False)
```

```python
import math

import jax
import jax.numpy as jnp
from jax import lax
from jax.experimental import pallas as pl
from jax.experimental.pallas import tpu as pltpu
from jax.sharding import PartitionSpec as P

MEMB = 64
BLOCK = 256
SLOTS = 32
SHARDS = 32
NBLK = 64
CELLS = NBLK * BLOCK
CHUNKS = 16
PER = NBLK // CHUNKS
HALF = MEMB // 2
LINE = 9
STEP = 8
WIDTH = 4096

f32 = jnp.float32
bf16 = jnp.bfloat16
exact_mode = lax.Precision.HIGHEST
NT = (((1,), (1,)), ((), ()))


def iota(shape, dim):
    return lax.broadcasted_iota(jnp.int32, shape, dim)


def split(x):
    hi = x.astype(bf16)
    return hi, (x - hi.astype(f32)).astype(bf16)


def route_kernel(owner_ref, local_ref, offset_ref, count_ref, value_ref, var_ref, out_ref):
    for w in range(2):
        owner = owner_ref[w : w + 1, :]
        across = jnp.broadcast_to(owner, (128, 128))
        same = jnp.where((across == across.T) & (iota((128, 128), 0) < iota((128, 128), 1)), 1.0, 0.0)
        rank = jnp.sum(same, axis=0, keepdims=True).astype(jnp.int32)
        target = owner * 2 + rank // 4
        placer = jnp.where(iota((2 * SHARDS, 128), 0) == target, 1.0, 0.0).astype(bf16)
        live = iota((SLOTS, 128), 0) < count_ref[w : w + 1, :]
        precision = jnp.where(live, 1.0 / var_ref[w], 0.0)
        rows = jnp.concatenate(
            [precision, precision * value_ref[w], (local_ref[w : w + 1, :] * BLOCK + offset_ref[w]).astype(f32)],
            axis=0,
        )
        wide = jnp.concatenate(
            [
                jnp.where(rank % 4 == c, rows[SLOTS * q : SLOTS * q + SLOTS], 0.0)
                for q in range(3)
                for c in range(4)
            ],
            axis=0,
        )
        high = wide.astype(bf16)
        rest = wide - high.astype(f32)
        middle = rest.astype(bf16)
        low = (rest - middle.astype(f32)).astype(bf16)
        placed = sum(
            lax.dot_general(placer, part, NT, preferred_element_type=f32) for part in (low, middle, high)
        )
        for q in range(3):
            out_ref[:, q, 2 * w : 2 * w + 2, :] = placed[:, 128 * q : 128 * q + 128].reshape(SHARDS, 2, 128)


def center_kernel(ens_hbm, mean_ref, ens, sems):
    copies = [
        pltpu.make_async_copy(
            ens_hbm.at[i // 4, :, pl.ds(i % 4 * 4096, 4096)], ens.at[i // 4, :, pl.ds(i % 4 * 4096, 4096)], sems.at[i]
        )
        for i in range(8)
    ]
    for copy in copies:
        copy.start()
    for i in range(8):
        copies[i].wait()

        def some(step, carry):
            block = i % 4 * 16 + step * 8
            for k in range(8):
                where = pl.ds(pl.multiple_of((block + k) * BLOCK, BLOCK), BLOCK)
                members = ens[i // 4, :, where].astype(f32)
                mean_ref[i // 4, pl.ds(block + k, 1), :] = jnp.sum(members, axis=0, keepdims=True) * (1.0 / MEMB)
            return carry

        lax.fori_loop(0, 2, some, 0)


def gram_kernel(recv_ref, mean_ref, ens_hbm, out_ref, ens, sems, table, dense, scale, ratio, even, odd, sums):
    copies = [pltpu.make_async_copy(ens_hbm.at[w], ens.at[w], sems.at[w]) for w in range(2)]
    for copy in copies:
        copy.start()
    for q in range(3):
        table[q] = jnp.concatenate(
            [recv_ref[:, q, 2 * w : 2 * w + 2, :].reshape(2 * SHARDS, 128) for w in range(2)], axis=0
        ).T
    locals_ = []
    for c in range(4):
        held = jnp.floor(table[2, SLOTS * c : SLOTS * c + 1, :] * (1.0 / BLOCK))
        locals_.append(held)
        table[2, SLOTS * c : SLOTS * c + SLOTS, :] = table[2, SLOTS * c : SLOTS * c + SLOTS, :] - held * BLOCK

    def scatter(tile, carry):
        base = pl.multiple_of(tile * 32, 32)
        cells = (iota((32, 128), 0) + base).astype(f32)
        for c in range(4):
            acc_u = jnp.zeros((32, 128), f32)
            acc_t = jnp.zeros((32, 128), f32)
            for r in range(SLOTS * c, SLOTS * c + SLOTS):
                hit = table[2, r : r + 1, :] == cells
                acc_u += jnp.where(hit, table[0, r : r + 1, :], 0.0)
                acc_t += jnp.where(hit, table[1, r : r + 1, :], 0.0)
            dense[pl.ds(base, 32), 128 * c : 128 * c + 128] = acc_u
            dense[pl.ds(base + 256, 32), 128 * c : 128 * c + 128] = acc_t
        return carry

    lax.fori_loop(0, 8, scatter, 0)
    row, lane = iota((2 * NBLK, 128), 0), iota((2 * NBLK, 128), 1)
    ours = (row // NBLK) == (lane // NBLK)
    holder = jnp.concatenate(
        [jnp.where(ours & ((row % NBLK).astype(f32) == held), 1.0, 0.0) for held in locals_], axis=1
    ).astype(bf16)
    placed = sum(lax.dot_general(holder, part, NT, preferred_element_type=f32) for part in split(dense[...])[::-1])
    for w in range(2):
        total = placed[NBLK * w : NBLK * w + NBLK, :256]
        root = jnp.sqrt(total)
        scale[w] = root
        ratio[w] = jnp.where(
            total > 0.0, (placed[NBLK * w : NBLK * w + NBLK, 256:] - total * mean_ref[w]) / root, 0.0
        )
    row16 = iota((16, BLOCK), 0)

    def fill(ref, step):
        w = step // PER
        for k in range(CHUNKS):
            b = step % PER * CHUNKS + k
            here = slice(BLOCK * k, BLOCK * k + BLOCK)
            cells = ens[w, :, pl.ds(pl.multiple_of(b * BLOCK, BLOCK), BLOCK)].astype(f32)
            high, low = split((cells - mean_ref[w, pl.ds(b, 1), :]) * scale[w, pl.ds(b, 1), :])
            ref[16 : 16 + MEMB, here] = high
            ref[16 + MEMB :, here] = low
            extra = ratio[w, pl.ds(b, 1), :]
            top = extra.astype(bf16).astype(f32)
            ref[0:16, here] = jnp.where(row16 == 0, top, jnp.where(row16 == 1, extra - top, 0.0)).astype(bf16)

    def product(ref, step):
        w = step // PER
        sums[w] = sums[w] + lax.dot_general(ref[16:, :], ref[: MEMB + 16, :], NT, preferred_element_type=f32)

    def steps(i, carry):
        product(even, 2 * i)
        fill(odd, 2 * i + 1)
        product(odd, 2 * i + 1)
        fill(even, jnp.minimum(2 * i + 2, 2 * PER - 1))
        return carry

    sums[...] = jnp.zeros((2, 2 * MEMB, MEMB + 16), f32)
    for copy in copies:
        copy.wait()
    fill(even, 0)
    lax.fori_loop(0, PER, steps, 0)
    row, col = iota((MEMB, MEMB), 0), iota((MEMB, MEMB), 1)
    lines = []
    for w in range(2):
        full = sums[w]
        cross = full[MEMB:, 16:]
        gram = full[:MEMB, 16:] + (cross + cross.T)
        both = full[:MEMB] + full[MEMB:]
        proj = jnp.sum(jnp.where(row == col, both[:, :1] + both[:, 1:2], 0.0), axis=0, keepdims=True)
        diag = jnp.sum(jnp.where(row == col, gram, 0.0), axis=0, keepdims=True)
        mixed = jnp.where(row[:HALF, :HALF] <= col[:HALF, :HALF], gram[:HALF, :HALF], gram[HALF:, HALF:])
        halves = jnp.concatenate([mixed, gram[:HALF, HALF:]], axis=1)
        body = jnp.concatenate([halves[:16], halves[16:]], axis=1)
        last = jnp.concatenate([proj, diag], axis=1)
        rows = [body[r : r + 1] for r in range(16)] + [last, jnp.zeros((1, 128), f32)]
        lines.append(
            jnp.concatenate([jnp.concatenate([rows[r], rows[r + LINE]], axis=0) for r in range(LINE)], axis=1)
        )
    for d in range(SHARDS):
        out_ref[d] = lines[d % 2]


def eliminate(systems):
    row, lane = iota((MEMB, 2 * MEMB), 0), iota((MEMB, 2 * MEMB), 1)
    eye = jnp.where(row + MEMB == lane, 1.0, 0.0)
    count = len(systems)
    tiles = []
    for system in systems:
        wide = jnp.concatenate([system, jnp.zeros((MEMB, MEMB), f32)], axis=1) + eye
        tiles.append([wide[8 * i : 8 * i + 8] for i in range(MEMB // 8)])
    found = [[] for _ in systems]
    full = (8, 2 * MEMB)
    for j in range(0, MEMB, STEP):
        t, s = divmod(j, 8)
        for w in range(count):
            rows = [jnp.broadcast_to(tiles[w][t][s + k : s + k + 1, :], full) for k in range(STEP)]
            block = [
                [jnp.broadcast_to(rows[k][:, j + l : j + l + 1], full) if l >= k else None for l in range(STEP)]
                for k in range(STEP)
            ]
            inverses, lower = [], [[None] * STEP for _ in range(STEP)]
            for k in range(STEP):
                inv = 1.0 / block[k][k]
                inverses.append(inv)
                for l in range(k + 1, STEP):
                    lower[l][k] = block[k][l] * inv
                for l in range(k + 1, STEP):
                    for m in range(l, STEP):
                        block[l][m] = block[l][m] - lower[l][k] * block[k][m]
                    rows[l] = rows[l] - lower[l][k] * rows[k]
            for k in range(STEP):
                found[w].append(rows[k][:1, :] * lax.rsqrt(block[k][k][:1, :]))
            first = t if s + STEP < 8 else t + 1
            if first == MEMB // 8:
                continue
            solved = [None] * STEP
            for k in reversed(range(STEP)):
                value = rows[k] * inverses[k]
                for l in range(k + 1, STEP):
                    value = value - lower[l][k] * solved[l]
                solved[k] = value
            for i in range(first, MEMB // 8):
                tile = tiles[w][i]
                change = None
                for k in range(STEP):
                    part = jnp.broadcast_to(tile[:, j + k : j + k + 1], full) * solved[k]
                    change = part if change is None else change + part
                tiles[w][i] = tile - change
    return [jnp.concatenate(rows, axis=0)[:, MEMB:] for rows in found]


def transform_kernel(infl_ref, parts_ref, out_ref):
    total = jnp.sum(parts_ref[...], axis=0)
    rows = [total[p : p + 1, 128 * r : 128 * r + 128] for p in range(2) for r in range(LINE)]
    body = jnp.concatenate(rows[:16], axis=0)
    proj = rows[16][:, :MEMB]
    halves = jnp.concatenate([body[:, :MEMB], body[:, MEMB:]], axis=0)
    mixed, corner = halves[:, :HALF], halves[:, HALF:]
    other = mixed.T
    row, col = iota((HALF, HALF), 0), iota((HALF, HALF), 1)
    diag = jnp.where(row == col, rows[16][:, MEMB + HALF :], 0.0)
    upper = jnp.where(row <= col, mixed, other)
    under = jnp.where(row > col, mixed, jnp.where(row < col, other, diag))
    gram = jnp.concatenate(
        [jnp.concatenate([upper, corner], axis=1), jnp.concatenate([corner.T, under], axis=1)], axis=0
    )
    ridge = jnp.where(iota((MEMB, MEMB), 0) == iota((MEMB, MEMB), 1), MEMB - 1.0, 0.0)
    inverse = eliminate([gram + ridge])[0]
    half = jnp.sum(inverse * proj, axis=1, keepdims=True)
    weight = jnp.sum(inverse * half, axis=0, keepdims=True)
    inner = weight + (infl_ref[lax.axis_index("space") & 1] * math.sqrt(MEMB - 1.0)) * inverse
    out_ref[...] = 1.0 / MEMB + inner - jnp.sum(inner, axis=1, keepdims=True) * (1.0 / MEMB)


def exact(a, b):
    return jnp.dot(a, b, precision=exact_mode, preferred_element_type=f32)


def apply_kernel(suffix_ref, first_ref, second_ref, ens_hbm, out_hbm, ens, out, in_sems, out_sems):
    pieces = 16384 // WIDTH

    def part(i):
        return (i // pieces, slice(None), pl.ds(i % pieces * WIDTH, WIDTH))

    reads = [pltpu.make_async_copy(ens_hbm.at[part(i)], ens.at[i], in_sems.at[i]) for i in range(2 * pieces)]
    for copy in reads:
        copy.start()
    last = exact(suffix_ref[...], second_ref[...])
    totals = [exact(last, first_ref[...]), last]
    writes = []
    for i in range(2 * pieces):
        reads[i].wait()
        both = jnp.concatenate(split(totals[i // pieces]), axis=1)
        cells = ens[i]
        out[i] = jnp.dot(both, jnp.concatenate([cells, cells], axis=0), preferred_element_type=f32)
        writes.append(pltpu.make_async_copy(out.at[i], out_hbm.at[part(i)], out_sems.at[i]))
        writes[i].start()
    for copy in writes:
        copy.wait()


def times(a, b):
    return jnp.matmul(a, b, precision=exact_mode)


def body(ensemble, obs_owner, obs_local, obs_offset, obs_count, obs_value, obs_var, inflation):
    vmem = pl.BlockSpec(memory_space=pltpu.VMEM)
    turned = lambda a: jnp.swapaxes(a, 1, 2)
    routed = pl.pallas_call(
        route_kernel,
        out_shape=pltpu.VMEM((SHARDS, 3, 4, 128), f32),
        in_specs=[vmem] * 6,
        out_specs=vmem,
        name="route",
    )(obs_owner[:, :, 0], obs_local, turned(obs_offset), obs_count, turned(obs_value), turned(obs_var))
    recv = lax.all_to_all(routed, "space", split_axis=0, concat_axis=0, tiled=True)
    ensemble = pltpu.with_memory_space_constraint(ensemble, pltpu.HBM)
    means = pl.pallas_call(
        center_kernel,
        out_shape=pltpu.VMEM((2, NBLK, BLOCK), f32),
        in_specs=[pl.BlockSpec(memory_space=pl.ANY)],
        out_specs=vmem,
        scratch_shapes=[pltpu.VMEM((2, MEMB, CELLS), bf16), pltpu.SemaphoreType.DMA((8,))],
        compiler_params=pltpu.CompilerParams(vmem_limit_bytes=20 * 2**20),
        name="center",
    )(ensemble)
    partial = pl.pallas_call(
        gram_kernel,
        out_shape=pltpu.VMEM((SHARDS, 2, LINE * 128), f32),
        in_specs=[vmem, vmem, pl.BlockSpec(memory_space=pl.ANY)],
        out_specs=vmem,
        scratch_shapes=[
            pltpu.VMEM((2, MEMB, CELLS), bf16),
            pltpu.SemaphoreType.DMA((2,)),
            pltpu.VMEM((3, 128, 128), f32),
            pltpu.VMEM((512, 512), f32),
            pltpu.VMEM((2, NBLK, BLOCK), f32),
            pltpu.VMEM((2, NBLK, BLOCK), f32),
            pltpu.VMEM((2 * MEMB + 16, CHUNKS * BLOCK), bf16),
            pltpu.VMEM((2 * MEMB + 16, CHUNKS * BLOCK), bf16),
            pltpu.VMEM((2, 2 * MEMB, MEMB + 16), f32),
        ],
        compiler_params=pltpu.CompilerParams(vmem_limit_bytes=30 * 2**20),
        name="gram",
    )(recv, means, ensemble)
    parts = lax.all_to_all(partial, "space", split_axis=0, concat_axis=0, tiled=True)
    second = (lax.axis_index("space") & 1) == 1
    made = pl.pallas_call(
        transform_kernel,
        out_shape=pltpu.VMEM((MEMB, MEMB), f32),
        in_specs=[pl.BlockSpec(memory_space=pltpu.SMEM), vmem],
        out_specs=vmem,
        compiler_params=pltpu.CompilerParams(vmem_limit_bytes=20 * 2**20),
        name="transform",
    )(inflation, parts)
    paired = lax.ppermute(made, "space", [(i, i ^ 1) for i in range(SHARDS)])
    early, late = jnp.where(second, paired, made), jnp.where(second, made, paired)
    product = times(late, early)
    place = lax.axis_index("tm")
    y = place // 2
    eye = jnp.eye(MEMB, dtype=f32)
    other = lax.ppermute(product, "tm", [(i, i ^ 1) for i in range(8)])
    first = (place & 1) == 0
    ahead = jnp.where(first, other, eye)
    product = times(jnp.where(first, other, product), jnp.where(first, product, other))
    one, two, three = (lax.ppermute(product, "tm", [(i, i ^ (2 * d)) for i in range(8)]) for d in (1, 2, 3))
    nearest = jnp.where(y == 3, eye, jnp.where(y == 1, three, one))
    middle = jnp.where(y < 2, two, eye)
    farthest = jnp.where(y == 0, three, eye)
    suffix = times(times(farthest, middle), times(nearest, ahead))
    return pl.pallas_call(
        apply_kernel,
        out_shape=jax.ShapeDtypeStruct((2, MEMB, CELLS), f32),
        in_specs=[vmem, vmem, vmem, pl.BlockSpec(memory_space=pl.ANY)],
        out_specs=pl.BlockSpec(memory_space=pl.ANY),
        scratch_shapes=[
            pltpu.VMEM((2 * CELLS // WIDTH, MEMB, WIDTH), bf16),
            pltpu.VMEM((2 * CELLS // WIDTH, MEMB, WIDTH), f32),
            pltpu.SemaphoreType.DMA((2 * CELLS // WIDTH,)),
            pltpu.SemaphoreType.DMA((2 * CELLS // WIDTH,)),
        ],
        compiler_params=pltpu.CompilerParams(vmem_limit_bytes=30 * 2**20),
        name="apply",
    )(suffix, early, late, ensemble)


def solution(mesh):
    in_specs = (
        P("tm", None, "space"),
        P("tm", "space", None),
        P("tm", "space"),
        P("tm", "space", None),
        P("tm", "space"),
        P("tm", "space", None),
        P("tm", "space", None),
        P("tm"),
    )
    out_specs = P("tm", None, "space")
    return jax.shard_map(body, mesh=mesh, in_specs=in_specs, out_specs=out_specs, check_vma=False)
```

```python
import math

import jax
import jax.numpy as jnp
from jax import lax
from jax.experimental import pallas as pl
from jax.experimental.pallas import tpu as pltpu
from jax.sharding import PartitionSpec as P

MEMB = 64
BLOCK = 256
SLOTS = 32
SHARDS = 32
NBLK = 64
CELLS = NBLK * BLOCK
CHUNKS = 16
PER = NBLK // CHUNKS
HALF = MEMB // 2
LINE = 9
STEP = 8
PIECES = ((1, 0, 2048), (1, 2048, 2048), (1, 4096, 4096), (1, 8192, 8192), (0, 0, 8192), (0, 8192, 8192))

f32 = jnp.float32
bf16 = jnp.bfloat16
exact_mode = lax.Precision.HIGHEST
NT = (((1,), (1,)), ((), ()))


def iota(shape, dim):
    return lax.broadcasted_iota(jnp.int32, shape, dim)


def split(x):
    hi = x.astype(bf16)
    return hi, (x - hi.astype(f32)).astype(bf16)


def route_kernel(owner_ref, local_ref, offset_ref, count_ref, value_ref, var_ref, out_ref):
    for w in range(2):
        owner = owner_ref[w : w + 1, :]
        across = jnp.broadcast_to(owner, (128, 128))
        same = jnp.where((across == across.T) & (iota((128, 128), 0) < iota((128, 128), 1)), 1.0, 0.0)
        rank = jnp.sum(same, axis=0, keepdims=True).astype(jnp.int32)
        target = owner * 2 + rank // 4
        placer = jnp.where(iota((2 * SHARDS, 128), 0) == target, 1.0, 0.0).astype(bf16)
        live = iota((SLOTS, 128), 0) < count_ref[w : w + 1, :]
        precision = jnp.where(live, 1.0 / var_ref[w], 0.0)
        rows = jnp.concatenate(
            [precision, precision * value_ref[w], (local_ref[w : w + 1, :] * BLOCK + offset_ref[w]).astype(f32)],
            axis=0,
        )
        wide = jnp.concatenate(
            [
                jnp.where(rank % 4 == c, rows[SLOTS * q : SLOTS * q + SLOTS], 0.0)
                for q in range(3)
                for c in range(4)
            ],
            axis=0,
        )
        high = wide.astype(bf16)
        rest = wide - high.astype(f32)
        middle = rest.astype(bf16)
        low = (rest - middle.astype(f32)).astype(bf16)
        placed = sum(
            lax.dot_general(placer, part, NT, preferred_element_type=f32) for part in (low, middle, high)
        )
        for q in range(3):
            out_ref[:, q, 2 * w : 2 * w + 2, :] = placed[:, 128 * q : 128 * q + 128].reshape(SHARDS, 2, 128)


def center_kernel(ens_hbm, mean_ref, ens, sems):
    copies = [
        pltpu.make_async_copy(
            ens_hbm.at[i // 4, :, pl.ds(i % 4 * 4096, 4096)], ens.at[i // 4, :, pl.ds(i % 4 * 4096, 4096)], sems.at[i]
        )
        for i in range(8)
    ]
    for copy in copies:
        copy.start()
    for i in range(8):
        copies[i].wait()

        def some(step, carry):
            block = i % 4 * 16 + step * 8
            for k in range(8):
                where = pl.ds(pl.multiple_of((block + k) * BLOCK, BLOCK), BLOCK)
                members = ens[i // 4, :, where].astype(f32)
                mean_ref[i // 4, pl.ds(block + k, 1), :] = jnp.sum(members, axis=0, keepdims=True) * (1.0 / MEMB)
            return carry

        lax.fori_loop(0, 2, some, 0)


def gram_kernel(recv_ref, mean_ref, ens_hbm, out_ref, ens, sems, table, dense, scale, ratio, even, odd, sums):
    copies = [pltpu.make_async_copy(ens_hbm.at[w], ens.at[w], sems.at[w]) for w in range(2)]
    for copy in copies:
        copy.start()
    for q in range(3):
        table[q] = jnp.concatenate(
            [recv_ref[:, q, 2 * w : 2 * w + 2, :].reshape(2 * SHARDS, 128) for w in range(2)], axis=0
        ).T
    locals_ = []
    for c in range(4):
        held = jnp.floor(table[2, SLOTS * c : SLOTS * c + 1, :] * (1.0 / BLOCK))
        locals_.append(held)
        table[2, SLOTS * c : SLOTS * c + SLOTS, :] = table[2, SLOTS * c : SLOTS * c + SLOTS, :] - held * BLOCK

    def scatter(tile, carry):
        base = pl.multiple_of(tile * 32, 32)
        cells = (iota((32, 128), 0) + base).astype(f32)
        for c in range(4):
            acc_u = jnp.zeros((32, 128), f32)
            acc_t = jnp.zeros((32, 128), f32)
            for r in range(SLOTS * c, SLOTS * c + SLOTS):
                hit = table[2, r : r + 1, :] == cells
                acc_u += jnp.where(hit, table[0, r : r + 1, :], 0.0)
                acc_t += jnp.where(hit, table[1, r : r + 1, :], 0.0)
            dense[pl.ds(base, 32), 128 * c : 128 * c + 128] = acc_u
            dense[pl.ds(base + 256, 32), 128 * c : 128 * c + 128] = acc_t
        return carry

    lax.fori_loop(0, 8, scatter, 0)
    row, lane = iota((2 * NBLK, 128), 0), iota((2 * NBLK, 128), 1)
    ours = (row // NBLK) == (lane // NBLK)
    holder = jnp.concatenate(
        [jnp.where(ours & ((row % NBLK).astype(f32) == held), 1.0, 0.0) for held in locals_], axis=1
    ).astype(bf16)
    placed = sum(lax.dot_general(holder, part, NT, preferred_element_type=f32) for part in split(dense[...])[::-1])
    for w in range(2):
        total = placed[NBLK * w : NBLK * w + NBLK, :256]
        root = jnp.sqrt(total)
        scale[w] = root
        ratio[w] = jnp.where(
            total > 0.0, (placed[NBLK * w : NBLK * w + NBLK, 256:] - total * mean_ref[w]) / root, 0.0
        )
    row16 = iota((16, BLOCK), 0)

    def fill(ref, step):
        w = step // PER
        for k in range(CHUNKS):
            b = step % PER * CHUNKS + k
            here = slice(BLOCK * k, BLOCK * k + BLOCK)
            cells = ens[w, :, pl.ds(pl.multiple_of(b * BLOCK, BLOCK), BLOCK)].astype(f32)
            high, low = split((cells - mean_ref[w, pl.ds(b, 1), :]) * scale[w, pl.ds(b, 1), :])
            ref[16 : 16 + MEMB, here] = high
            ref[16 + MEMB :, here] = low
            extra = ratio[w, pl.ds(b, 1), :]
            top = extra.astype(bf16).astype(f32)
            ref[0:16, here] = jnp.where(row16 == 0, top, jnp.where(row16 == 1, extra - top, 0.0)).astype(bf16)

    def product(ref, step):
        w = step // PER
        sums[w] = sums[w] + lax.dot_general(ref[16:, :], ref[: MEMB + 16, :], NT, preferred_element_type=f32)

    def steps(i, carry):
        product(even, 2 * i)
        fill(odd, 2 * i + 1)
        product(odd, 2 * i + 1)
        fill(even, jnp.minimum(2 * i + 2, 2 * PER - 1))
        return carry

    sums[...] = jnp.zeros((2, 2 * MEMB, MEMB + 16), f32)
    for copy in copies:
        copy.wait()
    fill(even, 0)
    lax.fori_loop(0, PER, steps, 0)
    row, col = iota((MEMB, MEMB), 0), iota((MEMB, MEMB), 1)
    lines = []
    for w in range(2):
        full = sums[w]
        cross = full[MEMB:, 16:]
        gram = full[:MEMB, 16:] + (cross + cross.T)
        both = full[:MEMB] + full[MEMB:]
        proj = jnp.sum(jnp.where(row == col, both[:, :1] + both[:, 1:2], 0.0), axis=0, keepdims=True)
        diag = jnp.sum(jnp.where(row == col, gram, 0.0), axis=0, keepdims=True)
        mixed = jnp.where(row[:HALF, :HALF] <= col[:HALF, :HALF], gram[:HALF, :HALF], gram[HALF:, HALF:])
        halves = jnp.concatenate([mixed, gram[:HALF, HALF:]], axis=1)
        body = jnp.concatenate([halves[:16], halves[16:]], axis=1)
        last = jnp.concatenate([proj, diag], axis=1)
        rows = [body[r : r + 1] for r in range(16)] + [last, jnp.zeros((1, 128), f32)]
        lines.append(
            jnp.concatenate([jnp.concatenate([rows[r], rows[r + LINE]], axis=0) for r in range(LINE)], axis=1)
        )
    for d in range(SHARDS):
        out_ref[d] = lines[d % 2]


def eliminate(systems):
    row, lane = iota((MEMB, 2 * MEMB), 0), iota((MEMB, 2 * MEMB), 1)
    eye = jnp.where(row + MEMB == lane, 1.0, 0.0)
    count = len(systems)
    tiles = []
    for system in systems:
        wide = jnp.concatenate([system, jnp.zeros((MEMB, MEMB), f32)], axis=1) + eye
        tiles.append([wide[8 * i : 8 * i + 8] for i in range(MEMB // 8)])
    found = [[] for _ in systems]
    full = (8, 2 * MEMB)
    for j in range(0, MEMB, STEP):
        for w in range(count):
            rows = [jnp.broadcast_to(tiles[w][(j + k) // 8][(j + k) % 8][None], full) for k in range(STEP)]
            block = [
                [jnp.broadcast_to(rows[k][:, j + l : j + l + 1], full) if l >= k else None for l in range(STEP)]
                for k in range(STEP)
            ]
            inverses, lower = [], [[None] * STEP for _ in range(STEP)]
            for k in range(STEP):
                inv = 1.0 / block[k][k]
                inverses.append(inv)
                for l in range(k + 1, STEP):
                    lower[l][k] = block[k][l] * inv
                for l in range(k + 1, STEP):
                    for m in range(l, STEP):
                        block[l][m] = block[l][m] - lower[l][k] * block[k][m]
                    rows[l] = rows[l] - lower[l][k] * rows[k]
            for k in range(STEP):
                found[w].append(rows[k][:1, :] * lax.rsqrt(block[k][k][:1, :]))
            first = (j + STEP) // 8
            if first == MEMB // 8:
                continue
            solved = [None] * STEP
            for k in reversed(range(STEP)):
                value = rows[k] * inverses[k]
                for l in range(k + 1, STEP):
                    value = value - lower[l][k] * solved[l]
                solved[k] = value
            for i in range(first, MEMB // 8):
                tile = tiles[w][i]
                change = None
                for k in range(STEP):
                    part = jnp.broadcast_to(tile[:, j + k : j + k + 1], full) * solved[k]
                    change = part if change is None else change + part
                tiles[w][i] = tile - change
    return [jnp.concatenate(rows, axis=0)[:, MEMB:] for rows in found]


def transform_kernel(infl_ref, parts_ref, out_ref):
    total = jnp.sum(parts_ref[...], axis=0)
    rows = [total[p : p + 1, 128 * r : 128 * r + 128] for p in range(2) for r in range(LINE)]
    body = jnp.concatenate(rows[:16], axis=0)
    proj = rows[16][:, :MEMB]
    halves = jnp.concatenate([body[:, :MEMB], body[:, MEMB:]], axis=0)
    mixed, corner = halves[:, :HALF], halves[:, HALF:]
    other = mixed.T
    row, col = iota((HALF, HALF), 0), iota((HALF, HALF), 1)
    diag = jnp.where(row == col, rows[16][:, MEMB + HALF :], 0.0)
    upper = jnp.where(row <= col, mixed, other)
    under = jnp.where(row > col, mixed, jnp.where(row < col, other, diag))
    gram = jnp.concatenate(
        [jnp.concatenate([upper, corner], axis=1), jnp.concatenate([corner.T, under], axis=1)], axis=0
    )
    ridge = jnp.where(iota((MEMB, MEMB), 0) == iota((MEMB, MEMB), 1), MEMB - 1.0, 0.0)
    inverse = eliminate([gram + ridge])[0]
    half = jnp.sum(inverse * proj, axis=1, keepdims=True)
    weight = jnp.sum(inverse * half, axis=0, keepdims=True)
    odd = (lax.axis_index("space") & 1) == 1
    inflation = jnp.where(odd, infl_ref[:, 1:2], infl_ref[:, 0:1])
    inner = weight + (inflation * math.sqrt(MEMB - 1.0)) * inverse
    out_ref[...] = 1.0 / MEMB + inner - jnp.sum(inner, axis=1, keepdims=True) * (1.0 / MEMB)


def exact(a, b):
    return jnp.dot(a, b, precision=exact_mode, preferred_element_type=f32)


def fetch_kernel(after_ref, ens_hbm, out_ref, sems):
    copies = [pltpu.make_async_copy(ens_hbm.at[w], out_ref.at[w], sems.at[w]) for w in range(2)]
    for copy in copies:
        copy.start()
    for copy in copies:
        copy.wait()


def pair_kernel(made_ref, paired_ref, late_ref, product_ref):
    odd = (lax.axis_index("space") & 1) == 1
    late = jnp.where(odd, made_ref[...], paired_ref[...])
    late_ref[...] = late
    product_ref[...] = exact(late, jnp.where(odd, paired_ref[...], made_ref[...]))


def join_kernel(product_ref, other_ref, ahead_ref, joined_ref):
    earlier = (lax.axis_index("tm") & 1) == 0
    product, other = product_ref[...], other_ref[...]
    joined_ref[...] = exact(jnp.where(earlier, other, product), jnp.where(earlier, product, other))
    eye = jnp.where(iota((MEMB, MEMB), 0) == iota((MEMB, MEMB), 1), 1.0, 0.0)
    ahead_ref[...] = jnp.where(earlier, other, eye)


def apply_kernel(one_ref, two_ref, three_ref, first_ref, second_ref, ens_ref, out_hbm, out, sems):
    y = lax.axis_index("tm") // 2
    eye = jnp.where(iota((MEMB, MEMB), 0) == iota((MEMB, MEMB), 1), 1.0, 0.0)
    one, two, three = one_ref[...], two_ref[...], three_ref[...]
    nearest = jnp.where(y == 3, eye, jnp.where(y == 1, three, one))
    behind = exact(jnp.where(y == 0, three, eye), jnp.where(y < 2, two, eye))
    totals = [exact(behind, exact(nearest, ref[...])) for ref in (first_ref, second_ref)]
    writes = []
    for i, (w, start, width) in enumerate(PIECES):
        both = jnp.concatenate(split(totals[w]), axis=1)
        here = slice(start, start + width)
        cells = ens_ref[w, :, here]
        out[w, :, here] = jnp.dot(both, jnp.concatenate([cells, cells], axis=0), preferred_element_type=f32)
        writes.append(
            pltpu.make_async_copy(out.at[w, :, pl.ds(start, width)], out_hbm.at[w, :, pl.ds(start, width)], sems.at[i])
        )
        writes[i].start()
    for copy in writes:
        copy.wait()


def times(a, b):
    return jnp.matmul(a, b, precision=exact_mode)


def body(ensemble, obs_owner, obs_local, obs_offset, obs_count, obs_value, obs_var, inflation):
    vmem = pl.BlockSpec(memory_space=pltpu.VMEM)
    turned = lambda a: jnp.swapaxes(a, 1, 2)
    routed = pl.pallas_call(
        route_kernel,
        out_shape=pltpu.VMEM((SHARDS, 3, 4, 128), f32),
        in_specs=[vmem] * 6,
        out_specs=vmem,
        name="route",
    )(obs_owner[:, :, 0], obs_local, turned(obs_offset), obs_count, turned(obs_value), turned(obs_var))
    recv = lax.all_to_all(routed, "space", split_axis=0, concat_axis=0, tiled=True)
    ensemble = pltpu.with_memory_space_constraint(ensemble, pltpu.HBM)
    means = pl.pallas_call(
        center_kernel,
        out_shape=pltpu.VMEM((2, NBLK, BLOCK), f32),
        in_specs=[pl.BlockSpec(memory_space=pl.ANY)],
        out_specs=vmem,
        scratch_shapes=[pltpu.VMEM((2, MEMB, CELLS), bf16), pltpu.SemaphoreType.DMA((8,))],
        compiler_params=pltpu.CompilerParams(vmem_limit_bytes=20 * 2**20),
        name="center",
    )(ensemble)
    partial = pl.pallas_call(
        gram_kernel,
        out_shape=pltpu.VMEM((SHARDS, 2, LINE * 128), f32),
        in_specs=[vmem, vmem, pl.BlockSpec(memory_space=pl.ANY)],
        out_specs=vmem,
        scratch_shapes=[
            pltpu.VMEM((2, MEMB, CELLS), bf16),
            pltpu.SemaphoreType.DMA((2,)),
            pltpu.VMEM((3, 128, 128), f32),
            pltpu.VMEM((512, 512), f32),
            pltpu.VMEM((2, NBLK, BLOCK), f32),
            pltpu.VMEM((2, NBLK, BLOCK), f32),
            pltpu.VMEM((2 * MEMB + 16, CHUNKS * BLOCK), bf16),
            pltpu.VMEM((2 * MEMB + 16, CHUNKS * BLOCK), bf16),
            pltpu.VMEM((2, 2 * MEMB, MEMB + 16), f32),
        ],
        compiler_params=pltpu.CompilerParams(vmem_limit_bytes=30 * 2**20),
        name="gram",
    )(recv, means, ensemble)
    parts = lax.all_to_all(partial, "space", split_axis=0, concat_axis=0, tiled=True)
    made = pl.pallas_call(
        transform_kernel,
        out_shape=pltpu.VMEM((MEMB, MEMB), f32),
        in_specs=[vmem, vmem],
        out_specs=vmem,
        compiler_params=pltpu.CompilerParams(vmem_limit_bytes=20 * 2**20),
        name="transform",
    )(inflation[None], parts)
    paired = lax.ppermute(made, "space", [(i, i ^ 1) for i in range(SHARDS)])
    held = pl.pallas_call(
        fetch_kernel,
        out_shape=pltpu.VMEM((2, MEMB, CELLS), bf16),
        in_specs=[pl.BlockSpec(memory_space=pl.ANY)] * 2,
        out_specs=vmem,
        scratch_shapes=[pltpu.SemaphoreType.DMA((2,))],
        compiler_params=pltpu.CompilerParams(vmem_limit_bytes=4 * 2**20),
        name="fetch",
    )(made, ensemble)
    square = pltpu.VMEM((MEMB, MEMB), f32)
    small = pltpu.CompilerParams(vmem_limit_bytes=4 * 2**20)
    late, product = pl.pallas_call(
        pair_kernel,
        out_shape=(square, square),
        in_specs=[vmem] * 2,
        out_specs=(vmem, vmem),
        compiler_params=small,
        name="pair",
    )(made, paired)
    other = lax.ppermute(product, "tm", [(i, i ^ 1) for i in range(8)])
    ahead, joined = pl.pallas_call(
        join_kernel,
        out_shape=(square, square),
        in_specs=[vmem] * 2,
        out_specs=(vmem, vmem),
        compiler_params=small,
        name="join",
    )(product, other)
    turned_by = {}
    for name, bits in (("far", 6), ("middle", 4), ("near", 2)):
        turned_by[name] = lax.ppermute(joined, "tm", [(i, i ^ bits) for i in range(8)])
    one, two, three = turned_by["near"], turned_by["middle"], turned_by["far"]
    return pl.pallas_call(
        apply_kernel,
        out_shape=jax.ShapeDtypeStruct((2, MEMB, CELLS), f32),
        in_specs=[vmem] * 6,
        out_specs=pl.BlockSpec(memory_space=pl.ANY),
        scratch_shapes=[pltpu.VMEM((2, MEMB, CELLS), f32), pltpu.SemaphoreType.DMA((len(PIECES),))],
        compiler_params=pltpu.CompilerParams(vmem_limit_bytes=30 * 2**20),
        name="apply",
    )(one, two, three, times(ahead, product), times(ahead, late), held)


def solution(mesh):
    in_specs = (
        P("tm", None, "space"),
        P("tm", "space", None),
        P("tm", "space"),
        P("tm", "space", None),
        P("tm", "space"),
        P("tm", "space", None),
        P("tm", "space", None),
        P("tm"),
    )
    out_specs = P("tm", None, "space")
    return jax.shard_map(body, mesh=mesh, in_specs=in_specs, out_specs=out_specs, check_vma=False)
```

```python
import math

import jax
import jax.numpy as jnp
from jax import lax
from jax.experimental import pallas as pl
from jax.experimental.pallas import tpu as pltpu
from jax.sharding import PartitionSpec as P

MEMB = 64
BLOCK = 256
SLOTS = 32
SHARDS = 32
NBLK = 64
CELLS = NBLK * BLOCK
CHUNKS = 16
TILE = 32
PER = NBLK // CHUNKS
HALF = MEMB // 2
LINE = 9
STEP = 8
PIECES = ((1, 0, 2048), (1, 2048, 2048), (1, 4096, 4096), (1, 8192, 8192), (0, 0, 8192), (0, 8192, 8192))

f32 = jnp.float32
bf16 = jnp.bfloat16
exact_mode = lax.Precision.HIGHEST
NT = (((1,), (1,)), ((), ()))


def iota(shape, dim):
    return lax.broadcasted_iota(jnp.int32, shape, dim)


def split(x):
    hi = x.astype(bf16)
    return hi, (x - hi.astype(f32)).astype(bf16)


def route_kernel(owner_ref, local_ref, offset_ref, count_ref, value_ref, var_ref, out_ref):
    for w in range(2):
        owner = owner_ref[w : w + 1, :]
        across = jnp.broadcast_to(owner, (128, 128))
        same = jnp.where((across == across.T) & (iota((128, 128), 0) < iota((128, 128), 1)), 1.0, 0.0)
        rank = jnp.sum(same, axis=0, keepdims=True).astype(jnp.int32)
        target = owner * 2 + rank // 4
        placer = jnp.where(iota((2 * SHARDS, 128), 0) == target, 1.0, 0.0).astype(bf16)
        live = iota((SLOTS, 128), 0) < count_ref[w : w + 1, :]
        precision = jnp.where(live, 1.0 / var_ref[w], 0.0)
        offsets = offset_ref[w].astype(f32)
        weighted = precision * value_ref[w]
        totals = [jnp.zeros((SLOTS, 128), f32)] * 2
        for r in range(SLOTS):
            equal = offsets == offsets[r : r + 1, :]
            totals = [
                total + jnp.where(equal, part[r : r + 1, :], 0.0) for total, part in zip(totals, (precision, weighted))
            ]
        cells = (local_ref[w : w + 1, :] * BLOCK).astype(f32) + offsets
        rows = jnp.concatenate(totals + [cells], axis=0)
        wide = jnp.concatenate(
            [
                jnp.where(rank % 4 == c, rows[SLOTS * q : SLOTS * q + SLOTS], 0.0)
                for q in range(3)
                for c in range(4)
            ],
            axis=0,
        )
        high = wide.astype(bf16)
        rest = wide - high.astype(f32)
        middle = rest.astype(bf16)
        low = (rest - middle.astype(f32)).astype(bf16)
        placed = sum(
            lax.dot_general(placer, part, NT, preferred_element_type=f32) for part in (low, middle, high)
        )
        for q in range(3):
            out_ref[:, q, 2 * w : 2 * w + 2, :] = placed[:, 128 * q : 128 * q + 128].reshape(SHARDS, 2, 128)


def center_kernel(ens_hbm, mean_ref, ens, sems):
    copies = [
        pltpu.make_async_copy(
            ens_hbm.at[i // 4, :, pl.ds(i % 4 * 4096, 4096)], ens.at[i // 4, :, pl.ds(i % 4 * 4096, 4096)], sems.at[i]
        )
        for i in range(8)
    ]
    for copy in copies:
        copy.start()
    for i in range(8):
        copies[i].wait()

        def some(step, carry):
            block = i % 4 * 16 + step * 8
            for k in range(8):
                where = pl.ds(pl.multiple_of((block + k) * BLOCK, BLOCK), BLOCK)
                members = ens[i // 4, :, where].astype(f32)
                mean_ref[i // 4, pl.ds(block + k, 1), :] = jnp.sum(members, axis=0, keepdims=True) * (1.0 / MEMB)
            return carry

        lax.fori_loop(0, 2, some, 0)


def gram_kernel(recv_ref, mean_ref, ens_hbm, out_ref, ens, sems, table, dense, scale, ratio, even, odd, sums):
    copies = [pltpu.make_async_copy(ens_hbm.at[w], ens.at[w], sems.at[w]) for w in range(2)]
    for copy in copies:
        copy.start()
    for q in range(3):
        table[q] = jnp.concatenate(
            [recv_ref[:, q, 2 * w : 2 * w + 2, :].reshape(2 * SHARDS, 128) for w in range(2)], axis=0
        ).T
    locals_ = []
    for c in range(4):
        held = jnp.floor(table[2, SLOTS * c : SLOTS * c + 1, :] * (1.0 / BLOCK))
        locals_.append(held)
        table[2, SLOTS * c : SLOTS * c + SLOTS, :] = table[2, SLOTS * c : SLOTS * c + SLOTS, :] - held * BLOCK

    def scatter(tile, carry):
        base = pl.multiple_of(tile * TILE, TILE)
        cells = (iota((TILE, 128), 0) + base).astype(f32)
        for c in range(4):
            found_u = jnp.zeros((TILE, 128), f32)
            found_t = jnp.zeros((TILE, 128), f32)
            for r in range(SLOTS * c, SLOTS * c + SLOTS):
                hit = table[2, r : r + 1, :] == cells
                found_u = jnp.where(hit, table[0, r : r + 1, :], found_u)
                found_t = jnp.where(hit, table[1, r : r + 1, :], found_t)
            dense[pl.ds(base, TILE), 128 * c : 128 * c + 128] = found_u
            dense[pl.ds(base + 256, TILE), 128 * c : 128 * c + 128] = found_t
        return carry

    lax.fori_loop(0, BLOCK // TILE, scatter, 0)
    row, lane = iota((2 * NBLK, 128), 0), iota((2 * NBLK, 128), 1)
    ours = (row // NBLK) == (lane // NBLK)
    holder = jnp.concatenate(
        [jnp.where(ours & ((row % NBLK).astype(f32) == held), 1.0, 0.0) for held in locals_], axis=1
    ).astype(bf16)
    placed = sum(lax.dot_general(holder, part, NT, preferred_element_type=f32) for part in split(dense[...])[::-1])
    for w in range(2):
        total = placed[NBLK * w : NBLK * w + NBLK, :256]
        root = jnp.sqrt(total)
        scale[w] = root
        ratio[w] = jnp.where(
            total > 0.0, (placed[NBLK * w : NBLK * w + NBLK, 256:] - total * mean_ref[w]) / root, 0.0
        )
    row16 = iota((16, BLOCK), 0)

    def fill(ref, step):
        w = step // PER
        for k in range(CHUNKS):
            b = step % PER * CHUNKS + k
            here = slice(BLOCK * k, BLOCK * k + BLOCK)
            cells = ens[w, :, pl.ds(pl.multiple_of(b * BLOCK, BLOCK), BLOCK)].astype(f32)
            high, low = split((cells - mean_ref[w, pl.ds(b, 1), :]) * scale[w, pl.ds(b, 1), :])
            ref[16 : 16 + MEMB, here] = high
            ref[16 + MEMB :, here] = low
            extra = ratio[w, pl.ds(b, 1), :]
            top = extra.astype(bf16).astype(f32)
            ref[0:16, here] = jnp.where(row16 == 0, top, jnp.where(row16 == 1, extra - top, 0.0)).astype(bf16)

    def product(ref, step):
        w = step // PER
        sums[w] = sums[w] + lax.dot_general(ref[16:, :], ref[: MEMB + 16, :], NT, preferred_element_type=f32)

    def steps(i, carry):
        product(even, 2 * i)
        fill(odd, 2 * i + 1)
        product(odd, 2 * i + 1)
        fill(even, jnp.minimum(2 * i + 2, 2 * PER - 1))
        return carry

    sums[...] = jnp.zeros((2, 2 * MEMB, MEMB + 16), f32)
    for copy in copies:
        copy.wait()
    fill(even, 0)
    lax.fori_loop(0, PER, steps, 0)
    row, col = iota((MEMB, MEMB), 0), iota((MEMB, MEMB), 1)
    lines = []
    for w in range(2):
        full = sums[w]
        cross = full[MEMB:, 16:]
        gram = full[:MEMB, 16:] + (cross + cross.T)
        both = full[:MEMB] + full[MEMB:]
        proj = jnp.sum(jnp.where(row == col, both[:, :1] + both[:, 1:2], 0.0), axis=0, keepdims=True)
        diag = jnp.sum(jnp.where(row == col, gram, 0.0), axis=0, keepdims=True)
        mixed = jnp.where(row[:HALF, :HALF] <= col[:HALF, :HALF], gram[:HALF, :HALF], gram[HALF:, HALF:])
        halves = jnp.concatenate([mixed, gram[:HALF, HALF:]], axis=1)
        body = jnp.concatenate([halves[:16], halves[16:]], axis=1)
        last = jnp.concatenate([proj, diag], axis=1)
        rows = [body[r : r + 1] for r in range(16)] + [last, jnp.zeros((1, 128), f32)]
        lines.append(
            jnp.concatenate([jnp.concatenate([rows[r], rows[r + LINE]], axis=0) for r in range(LINE)], axis=1)
        )
    for d in range(SHARDS):
        out_ref[d] = lines[d % 2]


def eliminate(systems):
    row, lane = iota((MEMB, 2 * MEMB), 0), iota((MEMB, 2 * MEMB), 1)
    eye = jnp.where(row + MEMB == lane, 1.0, 0.0)
    count = len(systems)
    tiles = []
    for system in systems:
        wide = jnp.concatenate([system, jnp.zeros((MEMB, MEMB), f32)], axis=1) + eye
        tiles.append([wide[8 * i : 8 * i + 8] for i in range(MEMB // 8)])
    found = [[] for _ in systems]
    full = (8, 2 * MEMB)
    for j in range(0, MEMB, STEP):
        for w in range(count):
            rows = [jnp.broadcast_to(tiles[w][(j + k) // 8][(j + k) % 8][None], full) for k in range(STEP)]
            block = [
                [jnp.broadcast_to(rows[k][:, j + l : j + l + 1], full) if l >= k else None for l in range(STEP)]
                for k in range(STEP)
            ]
            inverses, lower = [], [[None] * STEP for _ in range(STEP)]
            for k in range(STEP):
                inv = 1.0 / block[k][k]
                inverses.append(inv)
                for l in range(k + 1, STEP):
                    lower[l][k] = block[k][l] * inv
                for l in range(k + 1, STEP):
                    for m in range(l, STEP):
                        block[l][m] = block[l][m] - lower[l][k] * block[k][m]
                    rows[l] = rows[l] - lower[l][k] * rows[k]
            for k in range(STEP):
                found[w].append(rows[k][:1, :] * lax.rsqrt(block[k][k][:1, :]))
            first = (j + STEP) // 8
            if first == MEMB // 8:
                continue
            solved = [None] * STEP
            for k in reversed(range(STEP)):
                value = rows[k] * inverses[k]
                for l in range(k + 1, STEP):
                    value = value - lower[l][k] * solved[l]
                solved[k] = value
            for i in range(first, MEMB // 8):
                tile = tiles[w][i]
                change = None
                for k in range(STEP):
                    part = jnp.broadcast_to(tile[:, j + k : j + k + 1], full) * solved[k]
                    change = part if change is None else change + part
                tiles[w][i] = tile - change
    return [jnp.concatenate(rows, axis=0)[:, MEMB:] for rows in found]


def transform_kernel(infl_ref, parts_ref, out_ref):
    total = jnp.sum(parts_ref[...], axis=0)
    rows = [total[p : p + 1, 128 * r : 128 * r + 128] for p in range(2) for r in range(LINE)]
    body = jnp.concatenate(rows[:16], axis=0)
    proj = rows[16][:, :MEMB]
    halves = jnp.concatenate([body[:, :MEMB], body[:, MEMB:]], axis=0)
    mixed, corner = halves[:, :HALF], halves[:, HALF:]
    other = mixed.T
    row, col = iota((HALF, HALF), 0), iota((HALF, HALF), 1)
    diag = jnp.where(row == col, rows[16][:, MEMB + HALF :], 0.0)
    upper = jnp.where(row <= col, mixed, other)
    under = jnp.where(row > col, mixed, jnp.where(row < col, other, diag))
    gram = jnp.concatenate(
        [jnp.concatenate([upper, corner], axis=1), jnp.concatenate([corner.T, under], axis=1)], axis=0
    )
    ridge = jnp.where(iota((MEMB, MEMB), 0) == iota((MEMB, MEMB), 1), MEMB - 1.0, 0.0)
    inverse = eliminate([gram + ridge])[0]
    half = jnp.sum(inverse * proj, axis=1, keepdims=True)
    weight = jnp.sum(inverse * half, axis=0, keepdims=True)
    odd = (lax.axis_index("space") & 1) == 1
    inflation = jnp.where(odd, infl_ref[:, 1:2], infl_ref[:, 0:1])
    inner = weight + (inflation * math.sqrt(MEMB - 1.0)) * inverse
    out_ref[...] = 1.0 / MEMB + inner - jnp.sum(inner, axis=1, keepdims=True) * (1.0 / MEMB)


def exact(a, b):
    return jnp.dot(a, b, precision=exact_mode, preferred_element_type=f32)


def fetch_kernel(after_ref, ens_hbm, out_ref, sems):
    copies = [pltpu.make_async_copy(ens_hbm.at[w], out_ref.at[w], sems.at[w]) for w in range(2)]
    for copy in copies:
        copy.start()
    for copy in copies:
        copy.wait()


def pair_kernel(made_ref, paired_ref, late_ref, product_ref):
    odd = (lax.axis_index("space") & 1) == 1
    late = jnp.where(odd, made_ref[...], paired_ref[...])
    late_ref[...] = late
    product_ref[...] = exact(late, jnp.where(odd, paired_ref[...], made_ref[...]))


def join_kernel(product_ref, other_ref, ahead_ref, joined_ref):
    earlier = (lax.axis_index("tm") & 1) == 0
    product, other = product_ref[...], other_ref[...]
    joined_ref[...] = exact(jnp.where(earlier, other, product), jnp.where(earlier, product, other))
    eye = jnp.where(iota((MEMB, MEMB), 0) == iota((MEMB, MEMB), 1), 1.0, 0.0)
    ahead_ref[...] = jnp.where(earlier, other, eye)


def apply_kernel(one_ref, two_ref, three_ref, first_ref, second_ref, ens_ref, out_hbm, out, sems):
    y = lax.axis_index("tm") // 2
    eye = jnp.where(iota((MEMB, MEMB), 0) == iota((MEMB, MEMB), 1), 1.0, 0.0)
    one, two, three = one_ref[...], two_ref[...], three_ref[...]
    nearest = jnp.where(y == 3, eye, jnp.where(y == 1, three, one))
    behind = exact(jnp.where(y == 0, three, eye), jnp.where(y < 2, two, eye))
    totals = [exact(behind, exact(nearest, ref[...])) for ref in (first_ref, second_ref)]
    writes = []
    for i, (w, start, width) in enumerate(PIECES):
        both = jnp.concatenate(split(totals[w]), axis=1)
        here = slice(start, start + width)
        cells = ens_ref[w, :, here]
        out[w, :, here] = jnp.dot(both, jnp.concatenate([cells, cells], axis=0), preferred_element_type=f32)
        writes.append(
            pltpu.make_async_copy(out.at[w, :, pl.ds(start, width)], out_hbm.at[w, :, pl.ds(start, width)], sems.at[i])
        )
        writes[i].start()
    for copy in writes:
        copy.wait()


def times(a, b):
    return jnp.matmul(a, b, precision=exact_mode)


def body(ensemble, obs_owner, obs_local, obs_offset, obs_count, obs_value, obs_var, inflation):
    vmem = pl.BlockSpec(memory_space=pltpu.VMEM)
    turned = lambda a: jnp.swapaxes(a, 1, 2)
    routed = pl.pallas_call(
        route_kernel,
        out_shape=pltpu.VMEM((SHARDS, 3, 4, 128), f32),
        in_specs=[vmem] * 6,
        out_specs=vmem,
        name="route",
    )(obs_owner[:, :, 0], obs_local, turned(obs_offset), obs_count, turned(obs_value), turned(obs_var))
    recv = lax.all_to_all(routed, "space", split_axis=0, concat_axis=0, tiled=True)
    ensemble = pltpu.with_memory_space_constraint(ensemble, pltpu.HBM)
    means = pl.pallas_call(
        center_kernel,
        out_shape=pltpu.VMEM((2, NBLK, BLOCK), f32),
        in_specs=[pl.BlockSpec(memory_space=pl.ANY)],
        out_specs=vmem,
        scratch_shapes=[pltpu.VMEM((2, MEMB, CELLS), bf16), pltpu.SemaphoreType.DMA((8,))],
        compiler_params=pltpu.CompilerParams(vmem_limit_bytes=20 * 2**20),
        name="center",
    )(ensemble)
    partial = pl.pallas_call(
        gram_kernel,
        out_shape=pltpu.VMEM((SHARDS, 2, LINE * 128), f32),
        in_specs=[vmem, vmem, pl.BlockSpec(memory_space=pl.ANY)],
        out_specs=vmem,
        scratch_shapes=[
            pltpu.VMEM((2, MEMB, CELLS), bf16),
            pltpu.SemaphoreType.DMA((2,)),
            pltpu.VMEM((3, 128, 128), f32),
            pltpu.VMEM((512, 512), f32),
            pltpu.VMEM((2, NBLK, BLOCK), f32),
            pltpu.VMEM((2, NBLK, BLOCK), f32),
            pltpu.VMEM((2 * MEMB + 16, CHUNKS * BLOCK), bf16),
            pltpu.VMEM((2 * MEMB + 16, CHUNKS * BLOCK), bf16),
            pltpu.VMEM((2, 2 * MEMB, MEMB + 16), f32),
        ],
        compiler_params=pltpu.CompilerParams(vmem_limit_bytes=30 * 2**20),
        name="gram",
    )(recv, means, ensemble)
    parts = lax.all_to_all(partial, "space", split_axis=0, concat_axis=0, tiled=True)
    made = pl.pallas_call(
        transform_kernel,
        out_shape=pltpu.VMEM((MEMB, MEMB), f32),
        in_specs=[vmem, vmem],
        out_specs=vmem,
        compiler_params=pltpu.CompilerParams(vmem_limit_bytes=20 * 2**20),
        name="transform",
    )(inflation[None], parts)
    paired = lax.ppermute(made, "space", [(i, i ^ 1) for i in range(SHARDS)])
    held = pl.pallas_call(
        fetch_kernel,
        out_shape=pltpu.VMEM((2, MEMB, CELLS), bf16),
        in_specs=[pl.BlockSpec(memory_space=pl.ANY)] * 2,
        out_specs=vmem,
        scratch_shapes=[pltpu.SemaphoreType.DMA((2,))],
        compiler_params=pltpu.CompilerParams(vmem_limit_bytes=4 * 2**20),
        name="fetch",
    )(made, ensemble)
    square = pltpu.VMEM((MEMB, MEMB), f32)
    small = pltpu.CompilerParams(vmem_limit_bytes=4 * 2**20)
    late, product = pl.pallas_call(
        pair_kernel,
        out_shape=(square, square),
        in_specs=[vmem] * 2,
        out_specs=(vmem, vmem),
        compiler_params=small,
        name="pair",
    )(made, paired)
    other = lax.ppermute(product, "tm", [(i, i ^ 1) for i in range(8)])
    ahead, joined = pl.pallas_call(
        join_kernel,
        out_shape=(square, square),
        in_specs=[vmem] * 2,
        out_specs=(vmem, vmem),
        compiler_params=small,
        name="join",
    )(product, other)
    turned_by = {}
    for name, bits in (("far", 6), ("middle", 4), ("near", 2)):
        turned_by[name] = lax.ppermute(joined, "tm", [(i, i ^ bits) for i in range(8)])
    one, two, three = turned_by["near"], turned_by["middle"], turned_by["far"]
    return pl.pallas_call(
        apply_kernel,
        out_shape=jax.ShapeDtypeStruct((2, MEMB, CELLS), f32),
        in_specs=[vmem] * 6,
        out_specs=pl.BlockSpec(memory_space=pl.ANY),
        scratch_shapes=[pltpu.VMEM((2, MEMB, CELLS), f32), pltpu.SemaphoreType.DMA((len(PIECES),))],
        compiler_params=pltpu.CompilerParams(vmem_limit_bytes=30 * 2**20),
        name="apply",
    )(one, two, three, times(ahead, product), times(ahead, late), held)


def solution(mesh):
    in_specs = (
        P("tm", None, "space"),
        P("tm", "space", None),
        P("tm", "space"),
        P("tm", "space", None),
        P("tm", "space"),
        P("tm", "space", None),
        P("tm", "space", None),
        P("tm"),
    )
    out_specs = P("tm", None, "space")
    return jax.shard_map(body, mesh=mesh, in_specs=in_specs, out_specs=out_specs, check_vma=False)
```

```python
import math

import jax
import jax.numpy as jnp
from jax import lax
from jax.experimental import pallas as pl
from jax.experimental.pallas import tpu as pltpu
from jax.sharding import PartitionSpec as P

MEMB = 64
BLOCK = 256
SLOTS = 32
SHARDS = 32
NBLK = 64
CELLS = NBLK * BLOCK
CHUNKS = 16
TILE = 32
PER = NBLK // CHUNKS
HALF = MEMB // 2
LINE = 9
STEP = 8
PIECES = ((1, 0, 2048), (1, 2048, 2048), (1, 4096, 4096), (1, 8192, 8192), (0, 0, 8192), (0, 8192, 8192))

f32 = jnp.float32
bf16 = jnp.bfloat16
exact_mode = lax.Precision.HIGHEST
NT = (((1,), (1,)), ((), ()))


def iota(shape, dim):
    return lax.broadcasted_iota(jnp.int32, shape, dim)


def split(x):
    hi = x.astype(bf16)
    return hi, (x - hi.astype(f32)).astype(bf16)


def route_kernel(owner_ref, local_ref, offset_ref, count_ref, value_ref, var_ref, out_ref):
    for w in range(2):
        owner = owner_ref[w : w + 1, :]
        across = jnp.broadcast_to(owner, (128, 128))
        same = jnp.where((across == across.T) & (iota((128, 128), 0) < iota((128, 128), 1)), 1.0, 0.0)
        rank = jnp.sum(same, axis=0, keepdims=True).astype(jnp.int32)
        target = owner * 2 + rank // 4
        placer = jnp.where(iota((2 * SHARDS, 128), 0) == target, 1.0, 0.0).astype(bf16)
        live = iota((SLOTS, 128), 0) < count_ref[w : w + 1, :]
        precision = jnp.where(live, 1.0 / var_ref[w], 0.0)
        offsets = offset_ref[w].astype(f32)
        weighted = precision * value_ref[w]
        totals = [jnp.zeros((SLOTS, 128), f32)] * 2
        for r in range(SLOTS):
            equal = offsets == offsets[r : r + 1, :]
            totals = [
                total + jnp.where(equal, part[r : r + 1, :], 0.0) for total, part in zip(totals, (precision, weighted))
            ]
        cells = (local_ref[w : w + 1, :] * BLOCK).astype(f32) + offsets
        rows = jnp.concatenate(totals + [cells], axis=0)
        wide = jnp.concatenate(
            [
                jnp.where(rank % 4 == c, rows[SLOTS * q : SLOTS * q + SLOTS], 0.0)
                for q in range(3)
                for c in range(4)
            ],
            axis=0,
        )
        high = wide.astype(bf16)
        rest = wide - high.astype(f32)
        middle = rest.astype(bf16)
        low = (rest - middle.astype(f32)).astype(bf16)
        placed = sum(
            lax.dot_general(placer, part, NT, preferred_element_type=f32) for part in (low, middle, high)
        )
        for q in range(3):
            out_ref[:, q, 2 * w : 2 * w + 2, :] = placed[:, 128 * q : 128 * q + 128].reshape(SHARDS, 2, 128)


def center_kernel(ens_hbm, mean_ref, ens, sems):
    copies = [
        pltpu.make_async_copy(
            ens_hbm.at[i // 4, :, pl.ds(i % 4 * 4096, 4096)], ens.at[i // 4, :, pl.ds(i % 4 * 4096, 4096)], sems.at[i]
        )
        for i in range(8)
    ]
    for copy in copies:
        copy.start()
    for i in range(8):
        copies[i].wait()

        def some(step, carry):
            block = i % 4 * 16 + step * 8
            for k in range(8):
                where = pl.ds(pl.multiple_of((block + k) * BLOCK, BLOCK), BLOCK)
                members = ens[i // 4, :, where].astype(f32)
                mean_ref[i // 4, pl.ds(block + k, 1), :] = jnp.sum(members, axis=0, keepdims=True) * (1.0 / MEMB)
            return carry

        lax.fori_loop(0, 2, some, 0)


def gram_kernel(recv_ref, mean_ref, ens_hbm, out_ref, ens, sems, table, dense, scale, ratio, even, odd, sums):
    copies = [pltpu.make_async_copy(ens_hbm.at[w], ens.at[w], sems.at[w]) for w in range(2)]
    for copy in copies:
        copy.start()
    for q in range(3):
        table[q] = jnp.concatenate(
            [recv_ref[:, q, 2 * w : 2 * w + 2, :].reshape(2 * SHARDS, 128) for w in range(2)], axis=0
        ).T
    locals_ = []
    for c in range(4):
        held = jnp.floor(table[2, SLOTS * c : SLOTS * c + 1, :] * (1.0 / BLOCK))
        locals_.append(held)
        table[2, SLOTS * c : SLOTS * c + SLOTS, :] = table[2, SLOTS * c : SLOTS * c + SLOTS, :] - held * BLOCK

    def scatter(tile, carry):
        base = pl.multiple_of(tile * TILE, TILE)
        cells = (iota((TILE, 128), 0) + base).astype(f32)
        for c in range(4):
            found_u = jnp.zeros((TILE, 128), f32)
            found_t = jnp.zeros((TILE, 128), f32)
            for r in range(SLOTS * c, SLOTS * c + SLOTS):
                hit = table[2, r : r + 1, :] == cells
                found_u = jnp.where(hit, table[0, r : r + 1, :], found_u)
                found_t = jnp.where(hit, table[1, r : r + 1, :], found_t)
            dense[pl.ds(base, TILE), 128 * c : 128 * c + 128] = found_u
            dense[pl.ds(base + 256, TILE), 128 * c : 128 * c + 128] = found_t
        return carry

    lax.fori_loop(0, BLOCK // TILE, scatter, 0)
    row, lane = iota((2 * NBLK, 128), 0), iota((2 * NBLK, 128), 1)
    ours = (row // NBLK) == (lane // NBLK)
    holder = jnp.concatenate(
        [jnp.where(ours & ((row % NBLK).astype(f32) == held), 1.0, 0.0) for held in locals_], axis=1
    ).astype(bf16)
    placed = sum(lax.dot_general(holder, part, NT, preferred_element_type=f32) for part in split(dense[...])[::-1])
    for w in range(2):
        total = placed[NBLK * w : NBLK * w + NBLK, :256]
        root = jnp.sqrt(total)
        scale[w] = root
        ratio[w] = jnp.where(
            total > 0.0, (placed[NBLK * w : NBLK * w + NBLK, 256:] - total * mean_ref[w]) / root, 0.0
        )
    row16 = iota((16, BLOCK), 0)

    def fill(ref, step):
        w = step // PER
        for k in range(CHUNKS):
            b = step % PER * CHUNKS + k
            here = slice(BLOCK * k, BLOCK * k + BLOCK)
            cells = ens[w, :, pl.ds(pl.multiple_of(b * BLOCK, BLOCK), BLOCK)].astype(f32)
            high, low = split((cells - mean_ref[w, pl.ds(b, 1), :]) * scale[w, pl.ds(b, 1), :])
            ref[16 : 16 + MEMB, here] = high
            ref[16 + MEMB :, here] = low
            extra = ratio[w, pl.ds(b, 1), :]
            top = extra.astype(bf16).astype(f32)
            ref[0:16, here] = jnp.where(row16 == 0, top, jnp.where(row16 == 1, extra - top, 0.0)).astype(bf16)

    def product(ref, step):
        w = step // PER
        sums[w] = sums[w] + lax.dot_general(ref[16:, :], ref[: MEMB + 16, :], NT, preferred_element_type=f32)

    def steps(i, carry):
        product(even, 2 * i)
        fill(odd, 2 * i + 1)
        product(odd, 2 * i + 1)
        fill(even, jnp.minimum(2 * i + 2, 2 * PER - 1))
        return carry

    sums[...] = jnp.zeros((2, 2 * MEMB, MEMB + 16), f32)
    for copy in copies:
        copy.wait()
    fill(even, 0)
    lax.fori_loop(0, PER, steps, 0)
    row, col = iota((MEMB, MEMB), 0), iota((MEMB, MEMB), 1)
    lines = []
    for w in range(2):
        full = sums[w]
        cross = full[MEMB:, 16:]
        gram = full[:MEMB, 16:] + (cross + cross.T)
        both = full[:MEMB] + full[MEMB:]
        proj = jnp.sum(jnp.where(row == col, both[:, :1] + both[:, 1:2], 0.0), axis=0, keepdims=True)
        diag = jnp.sum(jnp.where(row == col, gram, 0.0), axis=0, keepdims=True)
        mixed = jnp.where(row[:HALF, :HALF] <= col[:HALF, :HALF], gram[:HALF, :HALF], gram[HALF:, HALF:])
        halves = jnp.concatenate([mixed, gram[:HALF, HALF:]], axis=1)
        body = jnp.concatenate([halves[:16], halves[16:]], axis=1)
        last = jnp.concatenate([proj, diag], axis=1)
        rows = [body[r : r + 1] for r in range(16)] + [last, jnp.zeros((1, 128), f32)]
        lines.append(
            jnp.concatenate([jnp.concatenate([rows[r], rows[r + LINE]], axis=0) for r in range(LINE)], axis=1)
        )
    for d in range(SHARDS):
        out_ref[d] = lines[d % 2]


def spread(tile, place):
    return jnp.take_along_axis(tile, jnp.full(tile.shape, place, jnp.int32), axis=1, mode="promise_in_bounds")


def eliminate(systems):
    row, lane = iota((MEMB, 2 * MEMB), 0), iota((MEMB, 2 * MEMB), 1)
    eye = jnp.where(row + MEMB == lane, 1.0, 0.0)
    count = len(systems)
    tiles = []
    for system in systems:
        wide = jnp.concatenate([system, jnp.zeros((MEMB, MEMB), f32)], axis=1) + eye
        tiles.append([wide[8 * i : 8 * i + 8] for i in range(MEMB // 8)])
    found = [[] for _ in systems]
    full = (8, 2 * MEMB)
    for j in range(0, MEMB, STEP):
        for w in range(count):
            rows = [jnp.broadcast_to(tiles[w][(j + k) // 8][(j + k) % 8][None], full) for k in range(STEP)]
            block = [
                [spread(rows[k], j + l) if l >= k else None for l in range(STEP)] for k in range(STEP)
            ]
            inverses, lower = [], [[None] * STEP for _ in range(STEP)]
            for k in range(STEP):
                inv = 1.0 / block[k][k]
                inverses.append(inv)
                for l in range(k + 1, STEP):
                    lower[l][k] = block[k][l] * inv
                for l in range(k + 1, STEP):
                    for m in range(l, STEP):
                        block[l][m] = block[l][m] - lower[l][k] * block[k][m]
                    rows[l] = rows[l] - lower[l][k] * rows[k]
            for k in range(STEP):
                found[w].append(rows[k][:1, :] * lax.rsqrt(block[k][k][:1, :]))
            first = (j + STEP) // 8
            if first == MEMB // 8:
                continue
            tile = tiles[w][first]
            columns = [spread(tile, j + k) for k in range(STEP)]
            for k in range(STEP):
                tile = tile - columns[k] * (rows[k] * inverses[k])
                for l in range(k + 1, STEP):
                    columns[l] = columns[l] - lower[l][k] * columns[k]
            tiles[w][first] = tile
            if first + 1 == MEMB // 8:
                continue
            solved = [None] * STEP
            for k in reversed(range(STEP)):
                value = rows[k] * inverses[k]
                for l in range(k + 1, STEP):
                    value = value - lower[l][k] * solved[l]
                solved[k] = value
            for i in range(first + 1, MEMB // 8):
                tile = tiles[w][i]
                change = None
                for k in range(STEP):
                    part = spread(tile, j + k) * solved[k]
                    change = part if change is None else change + part
                tiles[w][i] = tile - change
    return [jnp.concatenate(rows, axis=0)[:, MEMB:] for rows in found]


def transform_kernel(infl_ref, parts_ref, out_ref):
    total = jnp.sum(parts_ref[...], axis=0)
    rows = [total[p : p + 1, 128 * r : 128 * r + 128] for p in range(2) for r in range(LINE)]
    body = jnp.concatenate(rows[:16], axis=0)
    proj = rows[16][:, :MEMB]
    halves = jnp.concatenate([body[:, :MEMB], body[:, MEMB:]], axis=0)
    mixed, corner = halves[:, :HALF], halves[:, HALF:]
    other = mixed.T
    row, col = iota((HALF, HALF), 0), iota((HALF, HALF), 1)
    diag = jnp.where(row == col, rows[16][:, MEMB + HALF :], 0.0)
    upper = jnp.where(row <= col, mixed, other)
    under = jnp.where(row > col, mixed, jnp.where(row < col, other, diag))
    gram = jnp.concatenate(
        [jnp.concatenate([upper, corner], axis=1), jnp.concatenate([corner.T, under], axis=1)], axis=0
    )
    ridge = jnp.where(iota((MEMB, MEMB), 0) == iota((MEMB, MEMB), 1), MEMB - 1.0, 0.0)
    inverse = eliminate([gram + ridge])[0]
    half = jnp.sum(inverse * proj, axis=1, keepdims=True)
    weight = jnp.sum(inverse * half, axis=0, keepdims=True)
    odd = (lax.axis_index("space") & 1) == 1
    inflation = jnp.where(odd, infl_ref[:, 1:2], infl_ref[:, 0:1])
    inner = weight + (inflation * math.sqrt(MEMB - 1.0)) * inverse
    out_ref[...] = 1.0 / MEMB + inner - jnp.sum(inner, axis=1, keepdims=True) * (1.0 / MEMB)


def exact(a, b):
    return jnp.dot(a, b, precision=exact_mode, preferred_element_type=f32)


def fetch_kernel(after_ref, ens_hbm, out_ref, sems):
    copies = [pltpu.make_async_copy(ens_hbm.at[w], out_ref.at[w], sems.at[w]) for w in range(2)]
    for copy in copies:
        copy.start()
    for copy in copies:
        copy.wait()


def pair_kernel(made_ref, paired_ref, late_ref, product_ref):
    odd = (lax.axis_index("space") & 1) == 1
    late = jnp.where(odd, made_ref[...], paired_ref[...])
    late_ref[...] = late
    product_ref[...] = exact(late, jnp.where(odd, paired_ref[...], made_ref[...]))


def join_kernel(product_ref, other_ref, ahead_ref, joined_ref):
    earlier = (lax.axis_index("tm") & 1) == 0
    product, other = product_ref[...], other_ref[...]
    joined_ref[...] = exact(jnp.where(earlier, other, product), jnp.where(earlier, product, other))
    eye = jnp.where(iota((MEMB, MEMB), 0) == iota((MEMB, MEMB), 1), 1.0, 0.0)
    ahead_ref[...] = jnp.where(earlier, other, eye)


def apply_kernel(one_ref, two_ref, three_ref, first_ref, second_ref, ens_ref, out_hbm, out, sems):
    y = lax.axis_index("tm") // 2
    eye = jnp.where(iota((MEMB, MEMB), 0) == iota((MEMB, MEMB), 1), 1.0, 0.0)
    one, two, three = one_ref[...], two_ref[...], three_ref[...]
    nearest = jnp.where(y == 3, eye, jnp.where(y == 1, three, one))
    behind = exact(jnp.where(y == 0, three, eye), jnp.where(y < 2, two, eye))
    totals = [exact(behind, exact(nearest, ref[...])) for ref in (first_ref, second_ref)]
    writes = []
    for i, (w, start, width) in enumerate(PIECES):
        both = jnp.concatenate(split(totals[w]), axis=1)
        here = slice(start, start + width)
        cells = ens_ref[w, :, here]
        out[w, :, here] = jnp.dot(both, jnp.concatenate([cells, cells], axis=0), preferred_element_type=f32)
        writes.append(
            pltpu.make_async_copy(out.at[w, :, pl.ds(start, width)], out_hbm.at[w, :, pl.ds(start, width)], sems.at[i])
        )
        writes[i].start()
    for copy in writes:
        copy.wait()


def times(a, b):
    return jnp.matmul(a, b, precision=exact_mode)


def body(ensemble, obs_owner, obs_local, obs_offset, obs_count, obs_value, obs_var, inflation):
    vmem = pl.BlockSpec(memory_space=pltpu.VMEM)
    turned = lambda a: jnp.swapaxes(a, 1, 2)
    routed = pl.pallas_call(
        route_kernel,
        out_shape=pltpu.VMEM((SHARDS, 3, 4, 128), f32),
        in_specs=[vmem] * 6,
        out_specs=vmem,
        name="route",
    )(obs_owner[:, :, 0], obs_local, turned(obs_offset), obs_count, turned(obs_value), turned(obs_var))
    recv = lax.all_to_all(routed, "space", split_axis=0, concat_axis=0, tiled=True)
    ensemble = pltpu.with_memory_space_constraint(ensemble, pltpu.HBM)
    means = pl.pallas_call(
        center_kernel,
        out_shape=pltpu.VMEM((2, NBLK, BLOCK), f32),
        in_specs=[pl.BlockSpec(memory_space=pl.ANY)],
        out_specs=vmem,
        scratch_shapes=[pltpu.VMEM((2, MEMB, CELLS), bf16), pltpu.SemaphoreType.DMA((8,))],
        compiler_params=pltpu.CompilerParams(vmem_limit_bytes=20 * 2**20),
        name="center",
    )(ensemble)
    partial = pl.pallas_call(
        gram_kernel,
        out_shape=pltpu.VMEM((SHARDS, 2, LINE * 128), f32),
        in_specs=[vmem, vmem, pl.BlockSpec(memory_space=pl.ANY)],
        out_specs=vmem,
        scratch_shapes=[
            pltpu.VMEM((2, MEMB, CELLS), bf16),
            pltpu.SemaphoreType.DMA((2,)),
            pltpu.VMEM((3, 128, 128), f32),
            pltpu.VMEM((512, 512), f32),
            pltpu.VMEM((2, NBLK, BLOCK), f32),
            pltpu.VMEM((2, NBLK, BLOCK), f32),
            pltpu.VMEM((2 * MEMB + 16, CHUNKS * BLOCK), bf16),
            pltpu.VMEM((2 * MEMB + 16, CHUNKS * BLOCK), bf16),
            pltpu.VMEM((2, 2 * MEMB, MEMB + 16), f32),
        ],
        compiler_params=pltpu.CompilerParams(vmem_limit_bytes=30 * 2**20),
        name="gram",
    )(recv, means, ensemble)
    parts = lax.all_to_all(partial, "space", split_axis=0, concat_axis=0, tiled=True)
    made = pl.pallas_call(
        transform_kernel,
        out_shape=pltpu.VMEM((MEMB, MEMB), f32),
        in_specs=[vmem, vmem],
        out_specs=vmem,
        compiler_params=pltpu.CompilerParams(vmem_limit_bytes=20 * 2**20),
        name="transform",
    )(inflation[None], parts)
    paired = lax.ppermute(made, "space", [(i, i ^ 1) for i in range(SHARDS)])
    held = pl.pallas_call(
        fetch_kernel,
        out_shape=pltpu.VMEM((2, MEMB, CELLS), bf16),
        in_specs=[pl.BlockSpec(memory_space=pl.ANY)] * 2,
        out_specs=vmem,
        scratch_shapes=[pltpu.SemaphoreType.DMA((2,))],
        compiler_params=pltpu.CompilerParams(vmem_limit_bytes=4 * 2**20),
        name="fetch",
    )(made, ensemble)
    square = pltpu.VMEM((MEMB, MEMB), f32)
    small = pltpu.CompilerParams(vmem_limit_bytes=4 * 2**20)
    late, product = pl.pallas_call(
        pair_kernel,
        out_shape=(square, square),
        in_specs=[vmem] * 2,
        out_specs=(vmem, vmem),
        compiler_params=small,
        name="pair",
    )(made, paired)
    other = lax.ppermute(product, "tm", [(i, i ^ 1) for i in range(8)])
    ahead, joined = pl.pallas_call(
        join_kernel,
        out_shape=(square, square),
        in_specs=[vmem] * 2,
        out_specs=(vmem, vmem),
        compiler_params=small,
        name="join",
    )(product, other)
    turned_by = {}
    for name, bits in (("far", 6), ("middle", 4), ("near", 2)):
        turned_by[name] = lax.ppermute(joined, "tm", [(i, i ^ bits) for i in range(8)])
    one, two, three = turned_by["near"], turned_by["middle"], turned_by["far"]
    return pl.pallas_call(
        apply_kernel,
        out_shape=jax.ShapeDtypeStruct((2, MEMB, CELLS), f32),
        in_specs=[vmem] * 6,
        out_specs=pl.BlockSpec(memory_space=pl.ANY),
        scratch_shapes=[pltpu.VMEM((2, MEMB, CELLS), f32), pltpu.SemaphoreType.DMA((len(PIECES),))],
        compiler_params=pltpu.CompilerParams(vmem_limit_bytes=30 * 2**20),
        name="apply",
    )(one, two, three, times(ahead, product), times(ahead, late), held)


def solution(mesh):
    in_specs = (
        P("tm", None, "space"),
        P("tm", "space", None),
        P("tm", "space"),
        P("tm", "space", None),
        P("tm", "space"),
        P("tm", "space", None),
        P("tm", "space", None),
        P("tm"),
    )
    out_specs = P("tm", None, "space")
    return jax.shard_map(body, mesh=mesh, in_specs=in_specs, out_specs=out_specs, check_vma=False)
```
